32 devices in a mesh: runs: 2 (over y), gz: 4 (over x, core), gx: 4 (over z).
Axes of the slice: x: 2, y: 2, z: 4, core: 2. Of those that a mesh axis runs over, the one named last changes fastest.
Arguments:
- magnetic: float32 [3, 64, 64, 1024], P(None, 'gx', 'gz', 'runs'), parts along dimension 3, may hold values from -12 to 12
- friction: float32 [64], P('gz'), may hold values from 0.3 to 3
Outputs:
- relaxed: float32 [3, 64, 64, 1024], P(None, 'gx', 'gz', 'runs'), parts along dimension 3
- potential: float32 [3, 64, 64, 1024], P(None, 'gx', 'gz', 'runs'), parts along dimension 3
The draws below stay inside these ranges and needn't reach their ends.
There are 2 independent parts, one for each index of `runs`. The reference program is written for one: setup_inputs(seed, part) draws one part's arguments, and reference() takes and returns one part's arrays. A program takes and returns all parts, laid end to end along the dimension named above; an argument that names none is the same for every part. Nothing has to cross between parts.
All inputs are finite; a program needn't handle non-finite values.
Results may differ from the reference program's by a relative error of at most 0.00017.
Values sent between devices are 32-bit elements; how exact they have to be, the bound alone decides.
A program may use at most 64 MiB of HBM per device.

```python
import math
import jax
import jax.numpy as jnp

NY = 512
DESCENTS = 2
RELAX = 2
NX = 64
NZ = 64


def draw_magnetic(key, part):
    x_frac = jnp.arange(NX, dtype=jnp.float32) / (NX - 1)
    z_frac = jnp.arange(NZ, dtype=jnp.float32) / (NZ - 1)
    amplitude = 1.7 * jnp.exp(jnp.log(3.0) * (0.5 * x_frac[:, None, None] - z_frac[None, :, None]))
    base = jax.random.truncated_normal(key, -4.0, 4.0, (3, NX, NZ, NY), jnp.float32)
    return (base * amplitude[None]).astype(jnp.float32)


def steps_of(key, extent, pieces, low, high):
    def one(position, shards_of):
        draws = jax.random.uniform(jax.random.fold_in(jax.random.fold_in(key, 6), position), (shards_of,), jnp.float32, low / len(pieces), high / len(pieces))
        return jnp.repeat(jnp.exp(draws), extent[position] // shards_of).reshape((-1,) + (1,) * (len(extent) - position - 1))

    level = one(*pieces[0])
    for cut in pieces[1:]:
        level = level * one(*cut)
    return level


def setup_inputs(seed: int = 0, part: int = 0) -> dict:
    arg_keys = jax.random.split(jax.random.key(seed), 3)
    own_keys = jax.random.split(jax.random.fold_in(arg_keys[2], part), 3)
    magnetic = draw_magnetic(jax.random.fold_in(jax.random.fold_in(arg_keys[2], part), 71), part)
    friction = jnp.clip(jnp.exp(math.log(3.0) - 2.3025851 * jax.random.uniform(arg_keys[1], (NZ,), jnp.float32) ** steps_of(arg_keys[1], (NZ,), ((0, 4),), -0.2, 0.2)), 0.3, 3.0)
    return dict(magnetic=magnetic, friction=friction)


step_scale = 0.5
time_step = 0.2


def diff_x(padded):
    return 0.5 * (padded[..., 2:, 1:-1, :] - padded[..., :-2, 1:-1, :])


def diff_z(padded):
    return 0.5 * (padded[..., 1:-1, 2:, :] - padded[..., 1:-1, :-2, :])


def diff_y(padded):
    middle = padded[..., 1:-1, 1:-1, :]
    return 0.5 * (jnp.roll(middle, -1, axis=-1) - jnp.roll(middle, 1, axis=-1))


def interior(padded):
    return padded[..., 1:-1, 1:-1, :]


def curl_of(padded):
    return jnp.stack([diff_y(padded[2]) - diff_z(padded[1]), diff_z(padded[0]) - diff_x(padded[2]), diff_x(padded[1]) - diff_y(padded[0])])


def divergence(padded):
    return diff_x(padded[0]) + diff_y(padded[1]) + diff_z(padded[2])


def gradient(scalar):
    return jnp.stack([diff_x(scalar), diff_y(scalar), diff_z(scalar)])


def cross_product(left, right):
    return jnp.stack([left[1] * right[2] - left[2] * right[1], left[2] * right[0] - left[0] * right[2], left[0] * right[1] - left[1] * right[0]])


def dot_product(left, right):
    return left[0] * right[0] + left[1] * right[1] + left[2] * right[2]


def pad_rim(values, width):
    return jnp.pad(values, ((0, 0), (width, width), (width, width), (0, 0)))


def omega_parts(widened):
    current = curl_of(widened)
    spread = divergence(widened)
    middle = interior(widened)
    square = jnp.maximum(dot_product(middle, middle), 1.0)
    lorentz = cross_product(current, middle)
    omega_field = (lorentz - spread[None] * middle) / square[None]
    return omega_field, current, spread, lorentz, square


def descent_force(omega_rim, field_rim, omega_core, current, spread, field_core):
    twisted = curl_of(cross_product(omega_rim, field_rim))
    twisted = twisted - cross_product(omega_core, current)
    twisted = twisted - gradient(dot_product(omega_rim, field_rim))
    twisted = twisted + omega_core * spread[None]
    return twisted + dot_product(omega_core, omega_core)[None] * field_core


def reference(magnetic, friction):
    field_now = magnetic
    cell_count = NX * NZ * NY
    for sweep_step in range(DESCENTS):
        widened = pad_rim(field_now, 2)
        omega_rim, current_rim, spread_rim, lorentz_rim, square_rim = omega_parts(widened)
        field_rim = interior(widened)
        omega_core = interior(omega_rim)
        current = interior(current_rim)
        spread = interior(spread_rim)
        lorentz = interior(lorentz_rim)
        square = interior(square_rim)
        descent = descent_force(omega_rim, field_rim, omega_core, current, spread, field_now)
        density = dot_product(lorentz, lorentz) / square + spread * spread
        step_rate = step_scale * (jnp.sum(density) / cell_count) / (jnp.sum(dot_product(descent, descent)) / cell_count + 1e-6)
        field_now = field_now + step_rate * descent
    relaxed = field_now
    columns = jnp.stack([-relaxed[1], relaxed[0]])
    suffix = jnp.flip(jnp.cumsum(jnp.flip(columns, 2), axis=2), 2)
    potential = jnp.concatenate([suffix, jnp.zeros_like(suffix[:1])], 0)
    for sweep_step in range(RELAX):
        induced = curl_of(pad_rim(potential, 1))
        current = curl_of(pad_rim(induced, 1))
        square = jnp.maximum(dot_product(induced, induced), 1.0)
        velocity = cross_product(current, induced) / (friction[None, :, None] * square)[None]
        potential = potential + time_step * cross_product(velocity, induced)
    return relaxed, potential
```

```python
import functools
import math

import jax
import jax.numpy as jnp
from jax import lax
from jax.experimental import pallas as pl
from jax.experimental.pallas import tpu as pltpu
from jax.sharding import PartitionSpec as P

DESCENTS = 2
RELAX = 2
ROUNDS = 1 + (DESCENTS - 1) + RELAX
LANES = 128

step_scale = 0.5
time_step = 0.2

DIRS = ((-1, 0), (1, 0), (0, -1), (0, 1), (-1, -1), (-1, 1), (1, -1), (1, 1))
PARTS = ((((0, 3, True),),) * DESCENTS + (((1, 2, True), (0, 1, False)),) + (((1, 3, True), (0, 1, False)),) * (RELAX - 1))
ZCOMPS = (3,) * DESCENTS + (2,) + (3,) * (RELAX - 1)
OPP = (1, 0, 3, 2, 7, 6, 5, 4)


def cross(l, r):
    return [l[1] * r[2] - l[2] * r[1], l[2] * r[0] - l[0] * r[2], l[0] * r[1] - l[1] * r[0]]


def dot(l, r):
    return l[0] * r[0] + l[1] * r[1] + l[2] * r[2]


def differ(ref, comps, i, r0, rows, lane):
    nb = ref.shape[2]
    first, last = lane == 0, lane == LANES - 1
    mid = {c: [ref[c, i, b, pl.ds(r0, rows), :] for b in range(nb)] for c in comps}

    def dy(c, b):
        here = mid[c][b]
        nxt, prv = mid[c][(b + 1) % nb], mid[c][(b - 1) % nb]
        up = pltpu.roll(jnp.where(first, nxt, here), LANES - 1, 1)
        down = pltpu.roll(jnp.where(last, prv, here), 1, 1)
        return up - down

    def dx(c, b):
        return ref[c, i + 1, b, pl.ds(r0, rows), :] - ref[c, i - 1, b, pl.ds(r0, rows), :]

    def dz(c, b):
        return ref[c, i, b, pl.ds(r0 + 1, rows), :] - ref[c, i, b, pl.ds(r0 - 1, rows), :]

    return mid, dx, dy, dz


def relaxing(mid, dx, dy, dz, drag, b):
    B = [mid[c][b] for c in range(3)]
    J = [dy(2, b) - dz(1, b), dz(0, b) - dx(2, b), dx(1, b) - dy(0, b)]
    inv = (0.5 * time_step) / (drag * jnp.maximum(dot(B, B), 1.0))
    v = [u * inv for u in cross(J, B)]
    return cross(v, B)


def kernel(
    gxn, gzn, cx, cz, nb, mag, friction, out_r, pot, out_e, out_d,
    fld, fb, fb2, eb, fric, xr, zs, zr, cs, cr, ps, pr, ts, tr, above,
    xsend, xrecv, zsend, zrecv, ssem, rsem, psend, precv, tsend, trecv, insem, far,
):
    gx = lax.axis_index("gx")
    gz = lax.axis_index("gz")
    n = gxn * gzn
    me = gz * gxn + gx
    core = pl.ds(8, cz)
    rim = cz + 8
    f32 = jnp.float32

    def lanes(b):
        return pl.ds(b * LANES, LANES)

    def in_copy(b):
        return pltpu.make_async_copy(
            mag.at[:, :, :, lanes(b)], fld.at[:, pl.ds(2, cx), b, core, :], insem.at[b]
        )

    for b in range(nb):
        in_copy(b).start()
    fric_copy = pltpu.make_async_copy(friction, fric, insem.at[nb])
    fric_copy.start()

    barrier = pltpu.get_barrier_semaphore()

    def peer(j):
        other = (me + j) % n
        return {"gz": other // gxn, "gx": other % gxn}

    def exists(d):
        dx, dz = DIRS[d]
        tests = []
        if dx:
            tests.append(gx > 0 if dx < 0 else gx < gxn - 1)
        if dz:
            tests.append(gz > 0 if dz < 0 else gz < gzn - 1)
        return functools.reduce(jnp.logical_and, tests)

    around = sum(jnp.where(exists(d), 1, 0) for d in range(8))

    def greet(sem):
        for d, (dx, dz) in enumerate(DIRS):
            @pl.when(exists(d))
            def _(dx=dx, dz=dz):
                pl.semaphore_signal(
                    sem, inc=1, device_id={"gz": gz + dz, "gx": gx + dx}, device_id_type=pl.DeviceIdType.MESH
                )

    greet(barrier)

    waves = max(gxn, gzn) - 2

    def wave_send(p):
        if p < waves:
            greet(far.at[p % 2])

    def wave_take(p):
        if p < waves:
            pl.semaphore_wait(far.at[p % 2], around)

    for ref in (fld, pot):
        for c in range(3):
            for i in (0, 1, cx + 2, cx + 3):
                ref[c, i] = jnp.zeros(ref.shape[2:], f32)

        def clear(i, _):
            for c in range(3):
                for b in range(nb):
                    ref[c, i, b, 0:8, :] = jnp.zeros((8, LANES), f32)
                    ref[c, i, b, cz + 8 : cz + 16, :] = jnp.zeros((8, LANES), f32)
            return 0

        lax.fori_loop(2, cx + 2, clear, 0)

    for b in range(nb):
        in_copy(b).wait()

    def near(side):
        return 1 if side == 0 else 0

    def x_link(r, d, q, src, arriving):
        c0, c1, both = PARTS[r][q]
        slot = d if arriving else OPP[d]
        start = (2 if d == 0 else cx) + (0 if both else near(OPP[d]))
        first, count = (0, 2) if both else (near(slot), 1)
        return pltpu.make_async_remote_copy(
            src_ref=src.at[pl.ds(c0, c1 - c0), pl.ds(start, count), :, core, :],
            dst_ref=xr.at[r, slot, pl.ds(c0, c1 - c0), pl.ds(first, count)],
            send_sem=xsend.at[r % 2, d, q], recv_sem=xrecv.at[r, slot, q],
            device_id={"gz": gz, "gx": gx + DIRS[d][0]}, device_id_type=pl.DeviceIdType.MESH,
        )

    half = cx // 2

    def z_link(r, d, h, arriving):
        o = d if arriving else OPP[d]
        comps, planes = pl.ds(0, ZCOMPS[r]), pl.ds(h * half, half)
        return pltpu.make_async_remote_copy(
            src_ref=zs.at[r, d - 2, comps, planes], dst_ref=zr.at[r, o - 2, comps, planes],
            send_sem=zsend.at[r % 2, d - 2, h], recv_sem=zrecv.at[r, o - 2, h],
            device_id={"gz": gz + DIRS[d][1], "gx": gx}, device_id_type=pl.DeviceIdType.MESH,
        )

    def link(r, d, arriving):
        dx, dz = DIRS[d]
        o = d if arriving else OPP[d]
        return pltpu.make_async_remote_copy(
            src_ref=cs.at[r, d - 4], dst_ref=cr.at[r, o - 4], send_sem=ssem.at[r % 2, d], recv_sem=rsem.at[r, o],
            device_id={"gz": gz + dz, "gx": gx + dx}, device_id_type=pl.DeviceIdType.MESH,
        )

    def send_x(r, src):
        for d in (0, 1):
            @pl.when(exists(d))
            def _(d=d):
                for q in range(len(PARTS[r])):
                    x_link(r, d, q, src, False).start()

    def pack_plane(r, i, src):
        for c in range(ZCOMPS[r]):
            for b in range(nb):
                zs[r, 0, c, i - 2, 2 * b : 2 * b + 2, :] = src[c, i, b, 8:10, :]
                zs[r, 1, c, i - 2, 2 * b : 2 * b + 2, :] = src[c, i, b, cz + 6 : cz + 8, :]

    def pack_corners(r, src):
        for d in range(4, 8):
            dx, dz = DIRS[d]
            i = 2 if dx < 0 else cx + 1
            k = 8 if dz < 0 else cz + 7
            for c in range(3):
                for b in range(nb):
                    cs[r, d - 4, c, b : b + 1, :] = src[c, i, b, k : k + 1, :]

    def send_corners(r):
        for d in range(4, 8):
            @pl.when(exists(d))
            def _(d=d):
                link(r, d, False).start()

    def send_z(r, h):
        for d in (2, 3):
            @pl.when(exists(d))
            def _(d=d):
                z_link(r, d, h, False).start()

    def loop(low, high, do, unroll=1):
        def step(i, _):
            do(i)
            return 0

        lax.fori_loop(low, high, step, 0, unroll=unroll)

    def put(old, new, mu):
        return new if mu is None else old + mu * new

    def take_z(r, dst, mu, h):
        for d in (2, 3):
            @pl.when(exists(d))
            def _(d=d):
                z_link(r, d, h, True).wait_recv()
                row = 6 if d == 2 else cz + 8

                def unpack(i):
                    for c in range(ZCOMPS[r]):
                        for b in range(nb):
                            dst[c, i + 2, b, row : row + 2, :] = put(
                                dst[c, i + 2, b, row : row + 2, :], zr[r, d - 2, c, i, 2 * b : 2 * b + 2, :], mu
                            )

                loop(h * half, h * half + half, unpack, 2)
                z_link(r, d, h, False).wait_send()

    def inner_planes(r, dst, mu, do, acc, unroll=1):
        for h in range(2):
            take_z(r, dst, mu, h)
            low, high = (3, half + 1) if h == 0 else (half + 1, cx + 1)
            acc = lax.fori_loop(low, high, do, acc, unroll=unroll)
        return acc

    def later_planes(r, do, acc, unroll=3):
        acc = lax.fori_loop(4, half + 2, do, acc, unroll=unroll)
        send_z(r, 0)
        acc = lax.fori_loop(half + 2, cx, do, acc, unroll=unroll)
        send_z(r, 1)
        return acc

    def take_x(r, src, dst, mu):
        for d in (4, 5, 6, 7):
            dx, dz = DIRS[d]

            @pl.when(exists(d))
            def _(d=d, dx=dx, dz=dz):
                link(r, d, True).wait_recv()
                i = 1 if dx < 0 else cx + 2
                k = 7 if dz < 0 else cz + 8
                for c in range(3):
                    for b in range(nb):
                        dst[c, i, b, k : k + 1, :] = put(dst[c, i, b, k : k + 1, :], cr[r, d - 4, c, b : b + 1, :], mu)
                link(r, d, False).wait_send()

        for d in (0, 1):
            @pl.when(exists(d))
            def _(d=d):
                base = 0 if d == 0 else cx + 2
                for q, (c0, c1, both) in enumerate(PARTS[r]):
                    x_link(r, d, q, src, True).wait_recv()
                    for c in range(c0, c1):
                        for p in range(2) if both else (near(d),):
                            for b in range(nb):
                                dst[c, base + p, b, core, :] = put(
                                    dst[c, base + p, b, core, :], xr[r, d, c, p, b], mu
                                )

        for d in (0, 1):
            @pl.when(exists(d))
            def _(d=d):
                for q in range(len(PARTS[r])):
                    x_link(r, d, q, src, False).wait_send()

    def over_edges(do, acc, low, width, unroll=1):
        def step(j, acc):
            return do(low + j + jnp.where(j >= width, cx + 3 - 2 * low - 2 * width + 1, 0), acc)

        return lax.fori_loop(0, 2 * width, step, acc, unroll=unroll)

    def folded(v):
        total = v[0:8]
        for k in range(8, v.shape[0], 8):
            total = total + v[k : k + 8]
        return total

    lane_rim = lax.broadcasted_iota(jnp.int32, (rim, LANES), 1)
    row_rim = lax.broadcasted_iota(jnp.int32, (rim, LANES), 0)
    lane_core = lax.broadcasted_iota(jnp.int32, (cz, LANES), 1)
    row_core = lax.broadcasted_iota(jnp.int32, (cz, LANES), 0)
    rows_in = (row_rim >= 1) & (row_rim <= cz)

    def omega_plane(i, acc):
        mid, dx, dy, dz = differ(fld, (0, 1, 2), i, 7, rim, lane_rim)
        rows = pl.ds(7, rim)
        inner = rows_in & ((i >= 2) & (i < cx + 2))
        for b in range(nb):
            B = [mid[c][b] for c in range(3)]
            J = [
                0.5 * (dy(2, b) - dz(1, b)),
                0.5 * (dz(0, b) - dx(2, b)),
                0.5 * (dx(1, b) - dy(0, b)),
            ]
            D = 0.5 * (dx(0, b) + dy(1, b) + dz(2, b))
            square = dot(B, B)
            inv = 1.0 / jnp.maximum(square, 1.0)
            part = square * inv
            L = cross(J, B)
            Li = [u * inv for u in L]
            E = cross(Li, B)
            for c in range(3):
                eb[c, i, b, rows, :] = E[c]
            eb[3, i, b, rows, :] = D * part
            drive = dot(L, Li)
            dd = D * D
            scale = inv * (drive + (dd * part - dd))
            lj = cross(Li, J)
            for c in range(3):
                fb[c, i, b, rows, :] = scale * B[c] - lj[c]
            acc = acc + folded(jnp.where(inner, drive + dd, 0.0))
        return acc

    def force_plane(i, acc):
        mid, dx, dy, dz = differ(eb, (0, 1, 2, 3), i, 8, cz, lane_core)
        for b in range(nb):
            curl = [
                dy(2, b) - dz(1, b) + dx(3, b),
                dz(0, b) - dx(2, b) + dy(3, b),
                dx(1, b) - dy(0, b) + dz(3, b),
            ]
            F = [fb[c, i, b, core, :] + 0.5 * curl[c] for c in range(3)]
            for c in range(3):
                fb2[c, i, b, core, :] = F[c]
            acc = acc + folded(dot(F, F))
        return acc

    def psum_copy(s, slot, j):
        return pltpu.make_async_remote_copy(
            src_ref=ps.at[s], dst_ref=pr.at[s, slot], send_sem=psend.at[s], recv_sem=precv.at[s],
            device_id=peer(j), device_id_type=pl.DeviceIdType.MESH,
        )

    def send_sums(s, lsum, gsum):
        ps[s, 0:1, :] = jnp.sum(lsum, axis=0, keepdims=True)
        ps[s, 1:2, :] = jnp.sum(gsum, axis=0, keepdims=True)

        def go(j, _):
            psum_copy(s, me, j).start()
            return 0

        lax.fori_loop(1, n, go, 0, unroll=3)

    def take_sums(s):
        pr[s, me] = ps[s]
        others = pr.at[s, pl.ds(0, n - 1)]
        pltpu.make_async_copy(others, others, precv.at[s]).wait()
        total = functools.reduce(lambda t, k: t + pr[s, k], range(1, n), pr[s, 0])
        sums = jnp.sum(total, axis=1, keepdims=True) / (n * cx * cz * nb * LANES)
        return step_scale * sums[0:1] / (sums[1:2] + 1e-6)

    def left_sums(s):
        others = pr.at[s, pl.ds(0, n - 1)]
        pltpu.make_async_copy(others, others, psend.at[s]).wait()

    def suffix_plane(i, src, dst):
        for c, other, sign in ((0, 1, -1.0), (1, 0, 1.0)):
            for b in range(nb):
                v = sign * src[other, i, b, core, :]
                step = 1
                while step < cz:
                    v = v + jnp.where(row_core < cz - step, pltpu.roll(v, cz - step, 0), 0.0)
                    step *= 2
                dst[c, i, b, core, :] = v

    def column_plane(i, src, slot):
        for c in range(2):
            for b in range(nb):
                ts[slot, c, i - 2, b : b + 1, :] = src[c, i, b, 8:9, :]

    def column_copy(slot, k, dz):
        return pltpu.make_async_remote_copy(
            src_ref=ts.at[slot], dst_ref=tr.at[slot, k], send_sem=tsend.at[slot, k], recv_sem=trecv.at[slot, k],
            device_id={"gz": gz + dz, "gx": gx}, device_id_type=pl.DeviceIdType.MESH,
        )

    def send_columns(slot):
        for k in range(1, gzn):
            @pl.when(gz - k >= 0)
            def _(k=k):
                column_copy(slot, k - 1, -k).start()

    loop(2, cx + 2, lambda i: pack_plane(0, i, fld), 2)
    pack_corners(0, fld)
    pl.semaphore_wait(barrier, around)
    send_x(0, fld)
    send_z(0, 0)
    send_z(0, 1)
    send_corners(0)
    wave_send(0)
    loop(2, cx + 2, lambda i: suffix_plane(i, fld, pot))
    zero = jnp.zeros((8, LANES), f32)
    mu = None
    for s in range(DESCENTS):
        last = s == DESCENTS - 1
        lsum = inner_planes(s, fld, mu, omega_plane, zero)
        if s == 0:
            wave_take(0)
            wave_send(1)
        take_x(s, fld if s == 0 else fb2, fld, mu)
        lsum = over_edges(omega_plane, lsum, 1, 2)

        def force(i, acc):
            acc = force_plane(i, acc)
            if not last:
                pack_plane(s + 1, i, fb2)
            return acc

        gsum = over_edges(force, zero, 2, 2, 4)
        if not last:
            send_x(s + 1, fb2)
            pack_corners(s + 1, fb2)
            send_corners(s + 1)
            gsum = later_planes(s + 1, force, gsum)
        else:
            gsum = lax.fori_loop(4, cx, force, gsum, unroll=4)
        if s == 0:
            for p in range(1, waves):
                wave_take(p)
                wave_send(p + 1)
        send_sums(s, lsum, gsum)
        loop(2, cx + 2, lambda i: suffix_plane(i, fb2, eb))
        if last:
            loop(2, cx + 2, lambda i: column_plane(i, eb, 1), 2)
            send_columns(1)
        mu = take_sums(s)

        def update(i):
            for c in range(3):
                for b in range(nb):
                    fld[c, i, b, core, :] = fld[c, i, b, core, :] + mu * fb2[c, i, b, core, :]

        def advance(i):
            update(i)
            for c in range(2):
                for b in range(nb):
                    pot[c, i, b, core, :] = pot[c, i, b, core, :] + mu * eb[c, i, b, core, :]
            column_plane(i, pot, 0)

        if not last:
            loop(2, cx + 2, advance)
        if s == DESCENTS - 2:
            send_columns(0)

    above[...] = jnp.zeros(above.shape, f32)
    for k in range(1, gzn):
        @pl.when(gz + k < gzn)
        def _(k=k):
            column_copy(0, k - 1, k).wait_recv()
            column_copy(1, k - 1, k).wait_recv()

            def gather(i):
                for c in range(2):
                    above[c, i] = above[c, i] + (tr[0, k - 1, c, i] + mu * tr[1, k - 1, c, i])

            loop(0, cx, gather, 2)

    def lift(i, acc):
        for c in range(2):
            for b in range(nb):
                pot[c, i, b, core, :] = (pot[c, i, b, core, :] + mu * eb[c, i, b, core, :]) + above[
                    c, i - 2, b : b + 1, :
                ]
        for b in range(nb):
            pot[2, i, b, core, :] = jnp.zeros((cz, LANES), f32)
        pack_plane(DESCENTS, i, pot)
        return acc

    over_edges(lift, 0, 2, 2)
    send_x(DESCENTS, pot)
    later_planes(DESCENTS, lift, 0)
    pack_corners(DESCENTS, pot)
    send_corners(DESCENTS)
    def finish(i):
        for c in range(3):
            for b in range(nb):
                out_r[c, i - 2, :, lanes(b)] = fld[c, i, b, core, :] + mu * fb2[c, i, b, core, :]

    loop(2, cx + 2, finish)
    for slot in range(2):
        for k in range(1, gzn):
            @pl.when(gz - k >= 0)
            def _(slot=slot, k=k):
                column_copy(slot, k - 1, -k).wait_send()

    for s in range(DESCENTS):
        left_sums(s)
    fric_copy.wait()
    drag = jnp.zeros((cz, LANES), f32)
    for k in range(cz):
        drag = jnp.where(row_core == k, fric[k], drag)
    z_at = gz * cz + row_rim - 1
    z_in = (z_at >= 0) & (z_at < gzn * cz)

    def induced_plane(dst, i, acc):
        mid, dx, dy, dz = differ(pot, (0, 1, 2), i, 7, rim, lane_rim)
        x_at = gx * cx + i - 2
        factor = jnp.where(z_in & ((x_at >= 0) & (x_at < gxn * cx)), 0.5, 0.0)
        rows = pl.ds(7, rim)
        for b in range(nb):
            dst[0, i, b, rows, :] = factor * (dy(2, b) - dz(1, b))
            dst[1, i, b, rows, :] = factor * (dz(0, b) - dx(2, b))
            dst[2, i, b, rows, :] = factor * (dx(1, b) - dy(0, b))
        return acc

    def relax_plane(i, acc):
        mid, dx, dy, dz = differ(eb, (0, 1, 2), i, 8, cz, lane_core)
        for b in range(nb):
            w = relaxing(mid, dx, dy, dz, drag, b)
            for c in range(3):
                pot[c, i, b, core, :] = pot[c, i, b, core, :] + w[c]
        return acc

    out_d[...] = drag
    for s in range(RELAX):
        r = DESCENTS + s
        last = s == RELAX - 1
        induced = functools.partial(induced_plane, out_e if last else eb)
        inner_planes(r, pot, None, induced, 0, 2)
        take_x(r, pot, pot, None)
        over_edges(induced, 0, 1, 2, 4)
        if last:
            break

        def relax(i, acc):
            acc = relax_plane(i, acc)
            pack_plane(r + 1, i, pot)
            return acc

        over_edges(relax, 0, 2, 2, 4)
        send_x(r + 1, pot)
        pack_corners(r + 1, pot)
        send_corners(r + 1)
        later_planes(r + 1, relax, 0)


def finish_kernel(cx, cz, nb, rel, pot, induced, drag_ref, out_r, out_p, buf, sem, rsem):
    lane = lax.broadcasted_iota(jnp.int32, (cz, LANES), 1)
    drag = drag_ref[...]
    rel_copy = pltpu.make_async_copy(rel, out_r, rsem)
    rel_copy.start()
    step = math.gcd(cx, 4)

    def copy(k):
        planes = pl.ds(k * step, step)
        return pltpu.make_async_copy(buf.at[:, planes], out_p.at[:, planes], sem.at[k])

    def some(k, _):
        for j in range(step):
            i = k * step + j
            mid, dx, dy, dz = differ(induced, (0, 1, 2), i + 2, 8, cz, lane)
            for b in range(nb):
                w = relaxing(mid, dx, dy, dz, drag, b)
                for c in range(3):
                    buf[c, i, :, b * LANES : (b + 1) * LANES] = pot[c, i + 2, b, 8 : 8 + cz, :] + w[c]
        copy(k).start()
        return 0

    lax.fori_loop(0, cx // step, some, 0)
    for k in range(cx // step):
        copy(k).wait()
    rel_copy.wait()


def body(magnetic, friction):
    _, cx, cz, ny = magnetic.shape
    gxn, gzn = lax.axis_size("gx"), lax.axis_size("gz")
    nb = ny // LANES
    n = gxn * gzn
    full = (cx + 4, nb, cz + 16, LANES)
    VM = lambda *shape: pltpu.VMEM(shape, jnp.float32)
    DMA = lambda *shape: pltpu.SemaphoreType.DMA(shape)
    like = lambda *shape: jax.ShapeDtypeStruct(shape, jnp.float32)
    shape = like(*magnetic.shape)
    inner = pl.BlockSpec(memory_space=pltpu.VMEM)
    outer = pl.BlockSpec(memory_space=pltpu.HBM)
    stay = lambda x: pltpu.with_memory_space_constraint(x, pltpu.HBM)
    limit = 40 * 1024 * 1024
    relaxed, pot, induced, drag = pl.pallas_call(
        functools.partial(kernel, gxn, gzn, cx, cz, nb),
        out_shape=(shape, like(3, *full), like(3, *full), like(cz, LANES)),
        in_specs=[outer, outer],
        out_specs=(inner, inner, inner, inner),
        scratch_shapes=[
            VM(3, *full), VM(3, *full), VM(3, *full), VM(4, *full),
            pltpu.SMEM((cz,), jnp.float32),
            VM(ROUNDS, 2, 3, 2, nb, cz, LANES),
            VM(ROUNDS, 2, 3, cx, 2 * nb, LANES), VM(ROUNDS, 2, 3, cx, 2 * nb, LANES),
            VM(ROUNDS, 4, 3, nb, LANES), VM(ROUNDS, 4, 3, nb, LANES),
            VM(DESCENTS, 2, LANES), VM(DESCENTS, n, 2, LANES),
            VM(2, 2, cx, nb, LANES), VM(2, gzn, 2, cx, nb, LANES), VM(2, cx, nb, LANES),
            DMA(2, 2, 2), DMA(ROUNDS, 2, 2), DMA(2, 2, 2), DMA(ROUNDS, 2, 2),
            DMA(2, 8), DMA(ROUNDS, 8),
            DMA(DESCENTS), DMA(DESCENTS), DMA(2, gzn), DMA(2, gzn), DMA(nb + 1),
            pltpu.SemaphoreType.REGULAR((2,)),
        ],
        compiler_params=pltpu.CompilerParams(
            collective_id=0, has_side_effects=True, vmem_limit_bytes=limit
        ),
    )(stay(magnetic), stay(friction))
    return pl.pallas_call(
        functools.partial(finish_kernel, cx, cz, nb),
        out_shape=(shape, shape),
        in_specs=[inner] * 4,
        out_specs=(outer, outer),
        scratch_shapes=[VM(*magnetic.shape), DMA(cx // math.gcd(cx, 4)), pltpu.SemaphoreType.DMA],
        compiler_params=pltpu.CompilerParams(vmem_limit_bytes=limit),
    )(relaxed, pot, induced, drag)


def solution(mesh):
    return jax.shard_map(
        body,
        mesh=mesh,
        in_specs=(P(None, "gx", "gz", "runs"), P("gz")),
        out_specs=(P(None, "gx", "gz", "runs"), P(None, "gx", "gz", "runs")),
        check_vma=False,
    )
```

```python
import functools
import math

import jax
import jax.numpy as jnp
from jax import lax
from jax.experimental import pallas as pl
from jax.experimental.pallas import tpu as pltpu
from jax.sharding import PartitionSpec as P

DESCENTS = 2
RELAX = 2
ROUNDS = 1 + (DESCENTS - 1) + RELAX
LANES = 128

step_scale = 0.5
time_step = 0.2

DIRS = ((-1, 0), (1, 0), (0, -1), (0, 1), (-1, -1), (-1, 1), (1, -1), (1, 1))
PARTS = ((((0, 3, True),),) * DESCENTS + (((1, 2, True), (0, 1, False)),) + (((1, 3, True), (0, 1, False)),) * (RELAX - 1))
ZCOMPS = (3,) * DESCENTS + (2,) + (3,) * (RELAX - 1)
OPP = (1, 0, 3, 2, 7, 6, 5, 4)


def cross(l, r):
    return [l[1] * r[2] - l[2] * r[1], l[2] * r[0] - l[0] * r[2], l[0] * r[1] - l[1] * r[0]]


def dot(l, r):
    return l[0] * r[0] + l[1] * r[1] + l[2] * r[2]


def differ(ref, comps, i, r0, rows, lane):
    nb = ref.shape[2]
    first, last = lane == 0, lane == LANES - 1
    mid = {c: [ref[c, i, b, pl.ds(r0, rows), :] for b in range(nb)] for c in comps}

    def dy(c, b):
        here = mid[c][b]
        nxt, prv = mid[c][(b + 1) % nb], mid[c][(b - 1) % nb]
        up = pltpu.roll(jnp.where(first, nxt, here), LANES - 1, 1)
        down = pltpu.roll(jnp.where(last, prv, here), 1, 1)
        return up - down

    def dx(c, b):
        return ref[c, i + 1, b, pl.ds(r0, rows), :] - ref[c, i - 1, b, pl.ds(r0, rows), :]

    def dz(c, b):
        return ref[c, i, b, pl.ds(r0 + 1, rows), :] - ref[c, i, b, pl.ds(r0 - 1, rows), :]

    return mid, dx, dy, dz


def relaxing(mid, dx, dy, dz, drag, b):
    B = [mid[c][b] for c in range(3)]
    J = [dy(2, b) - dz(1, b), dz(0, b) - dx(2, b), dx(1, b) - dy(0, b)]
    inv = (0.5 * time_step) / (drag * jnp.maximum(dot(B, B), 1.0))
    v = [u * inv for u in cross(J, B)]
    return cross(v, B)


def kernel(
    gxn, gzn, cx, cz, nb, mag, friction, out_r, pot, out_e, out_d,
    fld, fb, fb2, eb, fric, xr, zs, zr, cs, cr, ps, pr, ts, tr, above,
    xsend, xrecv, zsend, zrecv, ssem, rsem, psend, precv, tsend, trecv, insem, far,
):
    gx = lax.axis_index("gx")
    gz = lax.axis_index("gz")
    n = gxn * gzn
    me = gz * gxn + gx
    core = pl.ds(8, cz)
    rim = cz + 8
    f32 = jnp.float32

    def lanes(b):
        return pl.ds(b * LANES, LANES)

    def in_copy(b):
        return pltpu.make_async_copy(
            mag.at[:, :, :, lanes(b)], fld.at[:, pl.ds(2, cx), b, core, :], insem.at[b]
        )

    for b in range(nb):
        in_copy(b).start()
    fric_copy = pltpu.make_async_copy(friction, fric, insem.at[nb])
    fric_copy.start()

    barrier = pltpu.get_barrier_semaphore()

    def peer(j):
        other = (me + j) % n
        return {"gz": other // gxn, "gx": other % gxn}

    def exists(d):
        dx, dz = DIRS[d]
        tests = []
        if dx:
            tests.append(gx > 0 if dx < 0 else gx < gxn - 1)
        if dz:
            tests.append(gz > 0 if dz < 0 else gz < gzn - 1)
        return functools.reduce(jnp.logical_and, tests)

    around = sum(jnp.where(exists(d), 1, 0) for d in range(8))

    def greet(sem):
        for d, (dx, dz) in enumerate(DIRS):
            @pl.when(exists(d))
            def _(dx=dx, dz=dz):
                pl.semaphore_signal(
                    sem, inc=1, device_id={"gz": gz + dz, "gx": gx + dx}, device_id_type=pl.DeviceIdType.MESH
                )

    greet(barrier)

    waves = max(gxn, gzn) - 2

    def wave_send(p):
        if p < waves:
            greet(far.at[p % 2])

    def wave_take(p):
        if p < waves:
            pl.semaphore_wait(far.at[p % 2], around)

    for ref in (fld, pot):
        for c in range(3):
            for i in (0, 1, cx + 2, cx + 3):
                ref[c, i] = jnp.zeros(ref.shape[2:], f32)

        def clear(i, _):
            for c in range(3):
                for b in range(nb):
                    ref[c, i, b, 0:8, :] = jnp.zeros((8, LANES), f32)
                    ref[c, i, b, cz + 8 : cz + 16, :] = jnp.zeros((8, LANES), f32)
            return 0

        lax.fori_loop(2, cx + 2, clear, 0)

    for b in range(nb):
        in_copy(b).wait()

    def near(side):
        return 1 if side == 0 else 0

    def x_link(r, d, q, src, arriving):
        c0, c1, both = PARTS[r][q]
        slot = d if arriving else OPP[d]
        start = (2 if d == 0 else cx) + (0 if both else near(OPP[d]))
        first, count = (0, 2) if both else (near(slot), 1)
        return pltpu.make_async_remote_copy(
            src_ref=src.at[pl.ds(c0, c1 - c0), pl.ds(start, count), :, core, :],
            dst_ref=xr.at[r, slot, pl.ds(c0, c1 - c0), pl.ds(first, count)],
            send_sem=xsend.at[r % 2, d, q], recv_sem=xrecv.at[r, slot, q],
            device_id={"gz": gz, "gx": gx + DIRS[d][0]}, device_id_type=pl.DeviceIdType.MESH,
        )

    half = cx // 2

    def z_link(r, d, h, arriving):
        o = d if arriving else OPP[d]
        comps, planes = pl.ds(0, ZCOMPS[r]), pl.ds(h * half, half)
        return pltpu.make_async_remote_copy(
            src_ref=zs.at[r, d - 2, comps, planes], dst_ref=zr.at[r, o - 2, comps, planes],
            send_sem=zsend.at[r % 2, d - 2, h], recv_sem=zrecv.at[r, o - 2, h],
            device_id={"gz": gz + DIRS[d][1], "gx": gx}, device_id_type=pl.DeviceIdType.MESH,
        )

    def link(r, d, arriving):
        dx, dz = DIRS[d]
        o = d if arriving else OPP[d]
        return pltpu.make_async_remote_copy(
            src_ref=cs.at[r, d - 4], dst_ref=cr.at[r, o - 4], send_sem=ssem.at[r % 2, d], recv_sem=rsem.at[r, o],
            device_id={"gz": gz + dz, "gx": gx + dx}, device_id_type=pl.DeviceIdType.MESH,
        )

    def send_x(r, src):
        for d in (0, 1):
            @pl.when(exists(d))
            def _(d=d):
                for q in range(len(PARTS[r])):
                    x_link(r, d, q, src, False).start()

    def pack_plane(r, i, src):
        for c in range(ZCOMPS[r]):
            for b in range(nb):
                zs[r, 0, c, i - 2, 2 * b : 2 * b + 2, :] = src[c, i, b, 8:10, :]
                zs[r, 1, c, i - 2, 2 * b : 2 * b + 2, :] = src[c, i, b, cz + 6 : cz + 8, :]

    def pack_corners(r, src):
        for d in range(4, 8):
            dx, dz = DIRS[d]
            i = 2 if dx < 0 else cx + 1
            k = 8 if dz < 0 else cz + 7
            for c in range(3):
                for b in range(nb):
                    cs[r, d - 4, c, b : b + 1, :] = src[c, i, b, k : k + 1, :]

    def send_corners(r):
        for d in range(4, 8):
            @pl.when(exists(d))
            def _(d=d):
                link(r, d, False).start()

    def send_z(r, h):
        for d in (2, 3):
            @pl.when(exists(d))
            def _(d=d):
                z_link(r, d, h, False).start()

    def loop(low, high, do, unroll=1):
        def step(i, _):
            do(i)
            return 0

        lax.fori_loop(low, high, step, 0, unroll=unroll)

    def put(old, new, mu):
        return new if mu is None else old + mu * new

    def take_z(r, dst, mu, h):
        for d in (2, 3):
            @pl.when(exists(d))
            def _(d=d):
                z_link(r, d, h, True).wait_recv()
                row = 6 if d == 2 else cz + 8

                def unpack(i):
                    for c in range(ZCOMPS[r]):
                        for b in range(nb):
                            dst[c, i + 2, b, row : row + 2, :] = put(
                                dst[c, i + 2, b, row : row + 2, :], zr[r, d - 2, c, i, 2 * b : 2 * b + 2, :], mu
                            )

                loop(h * half, h * half + half, unpack, 2)
                z_link(r, d, h, False).wait_send()

    def inner_planes(r, dst, mu, do, acc, unroll=1):
        for h in range(2):
            take_z(r, dst, mu, h)
            low, high = (3, half + 1) if h == 0 else (half + 1, cx + 1)
            acc = lax.fori_loop(low, high, do, acc, unroll=unroll)
        return acc

    def later_planes(r, do, acc, unroll=3):
        acc = lax.fori_loop(4, half + 2, do, acc, unroll=unroll)
        send_z(r, 0)
        acc = lax.fori_loop(half + 2, cx, do, acc, unroll=unroll)
        send_z(r, 1)
        return acc

    def take_x(r, src, dst, mu):
        for d in (4, 5, 6, 7):
            dx, dz = DIRS[d]

            @pl.when(exists(d))
            def _(d=d, dx=dx, dz=dz):
                link(r, d, True).wait_recv()
                i = 1 if dx < 0 else cx + 2
                k = 7 if dz < 0 else cz + 8
                if dst is not None:
                    for c in range(3):
                        for b in range(nb):
                            dst[c, i, b, k : k + 1, :] = put(
                                dst[c, i, b, k : k + 1, :], cr[r, d - 4, c, b : b + 1, :], mu
                            )
                link(r, d, False).wait_send()

        for d in (0, 1):
            @pl.when(exists(d))
            def _(d=d):
                base = 0 if d == 0 else cx + 2
                for q, (c0, c1, both) in enumerate(PARTS[r]):
                    x_link(r, d, q, src, True).wait_recv()
                    if dst is None:
                        continue
                    for c in range(c0, c1):
                        for p in range(2) if both else (near(d),):
                            for b in range(nb):
                                dst[c, base + p, b, core, :] = put(
                                    dst[c, base + p, b, core, :], xr[r, d, c, p, b], mu
                                )

        for d in (0, 1):
            @pl.when(exists(d))
            def _(d=d):
                for q in range(len(PARTS[r])):
                    x_link(r, d, q, src, False).wait_send()

    def over_edges(do, acc, low, width, unroll=1):
        def step(j, acc):
            return do(low + j + jnp.where(j >= width, cx + 3 - 2 * low - 2 * width + 1, 0), acc)

        return lax.fori_loop(0, 2 * width, step, acc, unroll=unroll)

    def folded(v):
        total = v[0:8]
        for k in range(8, v.shape[0], 8):
            total = total + v[k : k + 8]
        return total

    lane_rim = lax.broadcasted_iota(jnp.int32, (rim, LANES), 1)
    row_rim = lax.broadcasted_iota(jnp.int32, (rim, LANES), 0)
    lane_core = lax.broadcasted_iota(jnp.int32, (cz, LANES), 1)
    row_core = lax.broadcasted_iota(jnp.int32, (cz, LANES), 0)
    rows_in = (row_rim >= 1) & (row_rim <= cz)

    def omega_plane(i, acc):
        mid, dx, dy, dz = differ(fld, (0, 1, 2), i, 7, rim, lane_rim)
        rows = pl.ds(7, rim)
        inner = rows_in & ((i >= 2) & (i < cx + 2))
        for b in range(nb):
            B = [mid[c][b] for c in range(3)]
            J = [
                0.5 * (dy(2, b) - dz(1, b)),
                0.5 * (dz(0, b) - dx(2, b)),
                0.5 * (dx(1, b) - dy(0, b)),
            ]
            D = 0.5 * (dx(0, b) + dy(1, b) + dz(2, b))
            square = dot(B, B)
            inv = 1.0 / jnp.maximum(square, 1.0)
            part = square * inv
            L = cross(J, B)
            Li = [u * inv for u in L]
            E = cross(Li, B)
            for c in range(3):
                eb[c, i, b, rows, :] = E[c]
            eb[3, i, b, rows, :] = D * part
            drive = dot(L, Li)
            dd = D * D
            scale = inv * (drive + (dd * part - dd))
            lj = cross(Li, J)
            for c in range(3):
                fb[c, i, b, rows, :] = scale * B[c] - lj[c]
            acc = acc + folded(jnp.where(inner, drive + dd, 0.0))
        return acc

    def force_plane(i, acc):
        mid, dx, dy, dz = differ(eb, (0, 1, 2, 3), i, 8, cz, lane_core)
        for b in range(nb):
            curl = [
                dy(2, b) - dz(1, b) + dx(3, b),
                dz(0, b) - dx(2, b) + dy(3, b),
                dx(1, b) - dy(0, b) + dz(3, b),
            ]
            F = [fb[c, i, b, core, :] + 0.5 * curl[c] for c in range(3)]
            for c in range(3):
                fb2[c, i, b, core, :] = F[c]
            acc = acc + folded(dot(F, F))
        return acc

    def psum_copy(s, slot, j):
        return pltpu.make_async_remote_copy(
            src_ref=ps.at[s], dst_ref=pr.at[s, slot], send_sem=psend.at[s], recv_sem=precv.at[s],
            device_id=peer(j), device_id_type=pl.DeviceIdType.MESH,
        )

    def send_sums(s, lsum, gsum):
        ps[s, 0:1, :] = jnp.sum(lsum, axis=0, keepdims=True)
        ps[s, 1:2, :] = jnp.sum(gsum, axis=0, keepdims=True)

        def go(j, _):
            psum_copy(s, me, j).start()
            return 0

        lax.fori_loop(1, n, go, 0, unroll=3)

    def take_sums(s):
        pr[s, me] = ps[s]
        others = pr.at[s, pl.ds(0, n - 1)]
        pltpu.make_async_copy(others, others, precv.at[s]).wait()
        total = functools.reduce(lambda t, k: t + pr[s, k], range(1, n), pr[s, 0])
        sums = jnp.sum(total, axis=1, keepdims=True) / (n * cx * cz * nb * LANES)
        return step_scale * sums[0:1] / (sums[1:2] + 1e-6)

    def left_sums(s):
        others = pr.at[s, pl.ds(0, n - 1)]
        pltpu.make_async_copy(others, others, psend.at[s]).wait()

    def suffix_plane(i, src, dst):
        for c, other, sign in ((0, 1, -1.0), (1, 0, 1.0)):
            for b in range(nb):
                v = sign * src[other, i, b, core, :]
                step = 1
                while step < cz:
                    v = v + jnp.where(row_core < cz - step, pltpu.roll(v, cz - step, 0), 0.0)
                    step *= 2
                dst[c, i, b, core, :] = v

    def column_plane(i, src, slot):
        for c in range(2):
            for b in range(nb):
                ts[slot, c, i - 2, b : b + 1, :] = src[c, i, b, 8:9, :]

    SIDES = ((0, 0, cx, 2), (1, 0, 2, cx + 2), (-1, cx - 2, 2, 0))

    def column_copy(slot, k, part, arriving):
        dx, first, count, land = SIDES[part]
        dx, dz = (dx, k) if arriving else (-dx, -k)
        return pltpu.make_async_remote_copy(
            src_ref=ts.at[slot, :, pl.ds(first, count)], dst_ref=tr.at[slot, k - 1, :, pl.ds(land, count)],
            send_sem=tsend.at[slot, k - 1, part], recv_sem=trecv.at[slot, k - 1, part],
            device_id={"gz": gz + dz, "gx": gx + dx}, device_id_type=pl.DeviceIdType.MESH,
        )

    def column_is(k, part, arriving):
        dx = SIDES[part][0] if arriving else -SIDES[part][0]
        test = gz + k < gzn if arriving else gz - k >= 0
        if dx:
            test = jnp.logical_and(test, gx > 0 if dx < 0 else gx < gxn - 1)
        return test

    def columns(arriving, do):
        for k in range(1, gzn):
            for part in range(3):
                @pl.when(column_is(k, part, arriving))
                def _(k=k, part=part):
                    do(k, part)

    def send_columns(slot):
        columns(False, lambda k, part: column_copy(slot, k, part, False).start())

    loop(2, cx + 2, lambda i: pack_plane(0, i, fld), 2)
    pack_corners(0, fld)
    pl.semaphore_wait(barrier, around)
    send_x(0, fld)
    send_z(0, 0)
    send_z(0, 1)
    send_corners(0)
    wave_send(0)
    loop(2, cx + 2, lambda i: suffix_plane(i, fld, pot))
    zero = jnp.zeros((8, LANES), f32)
    mu = None
    for s in range(DESCENTS):
        last = s == DESCENTS - 1
        lsum = inner_planes(s, fld, mu, omega_plane, zero)
        if s == 0:
            wave_take(0)
            wave_send(1)
        take_x(s, fld if s == 0 else fb2, fld, mu)
        lsum = over_edges(omega_plane, lsum, 1, 2)

        def force(i, acc):
            acc = force_plane(i, acc)
            pack_plane(s + 1, i, fb2)
            return acc

        gsum = over_edges(force, zero, 2, 2, 4)
        suffix = lambda i: suffix_plane(i, fb2, fb)
        if last:
            over_edges(lambda i, acc: (suffix(i), acc)[1], 0, 2, 2, 2)
        gsum = lax.fori_loop(4, cx, force, gsum, unroll=4)
        pack_corners(s + 1, fb2)
        if s == 0:
            for p in range(1, waves):
                wave_take(p)
                wave_send(p + 1)
        send_sums(s, lsum, gsum)
        if not last:
            send_z(s + 1, 0)
            send_z(s + 1, 1)
            send_x(s + 1, fb if last else fb2)
            send_corners(s + 1)
        if last:
            loop(4, cx, suffix, 2)
            loop(2, cx + 2, lambda i: column_plane(i, fb, 1), 2)
            send_columns(1)
            send_z(s + 1, 0)
            send_z(s + 1, 1)
            send_x(s + 1, fb if last else fb2)
            send_corners(s + 1)
            over_edges(lambda i, acc: (suffix_plane(i, fld, pot), acc)[1], 0, 0, 2, 2)
            above[...] = jnp.zeros(above.shape, f32)
        else:
            loop(2, cx + 2, suffix, 2)
        mu = take_sums(s)

        def update(i):
            for c in range(3):
                for b in range(nb):
                    fld[c, i, b, core, :] = fld[c, i, b, core, :] + mu * fb2[c, i, b, core, :]

        def advance(i):
            update(i)
            for c in range(2):
                for b in range(nb):
                    pot[c, i, b, core, :] = pot[c, i, b, core, :] + mu * fb[c, i, b, core, :]
            column_plane(i, pot, 0)

        if not last:
            loop(2, cx + 2, advance)
        if s == DESCENTS - 2:
            send_columns(0)

    def gather(k, part):
        dx, first, count, land = SIDES[part]
        column_copy(0, k, part, True).wait_recv()
        column_copy(1, k, part, True).wait_recv()

        def one(i):
            for c in range(2):
                above[c, i] = above[c, i] + (tr[0, k - 1, c, i] + mu * tr[1, k - 1, c, i])

        loop(land, land + count, one, 2)

    columns(True, gather)
    take_x(DESCENTS, fb, None, None)

    def lift(i):
        for c in range(2):
            for b in range(nb):
                pot[c, i, b, core, :] = (pot[c, i, b, core, :] + mu * fb[c, i, b, core, :]) + above[c, i, b : b + 1, :]
        for b in range(nb):
            pot[2, i, b, core, :] = jnp.zeros((cz, LANES), f32)

    loop(2, cx + 2, lift, 2)
    for d in (0, 1):
        @pl.when(exists(d))
        def _(d=d):
            base = 0 if d == 0 else cx + 2
            for c, p in ((0, near(d)), (1, 0), (1, 1)):
                i = base + p
                for b in range(nb):
                    pot[c, i, b, core, :] = (
                        pot[c, i, b, core, :] + mu * xr[DESCENTS, d, c, p, b]
                    ) + above[c, i, b : b + 1, :]

    def below(c, i, b, rows, force):
        return (1.0 if c else -1.0) * (fld[1 - c, i, b, rows, :] + mu * force)

    for h in range(2):
        @pl.when(exists(2))
        def _(h=h):
            z_link(DESCENTS, 2, h, True).wait_recv()

            def low_rows(i):
                for c in range(2):
                    for b in range(nb):
                        g = below(c, i + 2, b, slice(6, 8), zr[DESCENTS, 0, 1 - c, i, 2 * b : 2 * b + 2, :])
                        row = pot[c, i + 2, b, 8:9, :] + g[1:2]
                        pot[c, i + 2, b, 7:8, :] = row
                        pot[c, i + 2, b, 6:7, :] = row + g[0:1]

            loop(h * half, h * half + half, low_rows)
            z_link(DESCENTS, 2, h, False).wait_send()

        @pl.when(exists(3))
        def _(h=h):
            z_link(DESCENTS, 3, h, True).wait_recv()

            def high_rows(i):
                for c in range(2):
                    for b in range(nb):
                        g = below(
                            c, i + 2, b, slice(cz + 8, cz + 9), zr[DESCENTS, 1, 1 - c, i, 2 * b : 2 * b + 1, :]
                        )
                        row = above[c, i + 2, b : b + 1, :]
                        pot[c, i + 2, b, cz + 8 : cz + 9, :] = row
                        pot[c, i + 2, b, cz + 9 : cz + 10, :] = row - g

            loop(h * half, h * half + half, high_rows)
            z_link(DESCENTS, 3, h, False).wait_send()

    for i, d in ((1, 4), (cx + 2, 6)):
        for c in range(2):
            for b in range(nb):
                pot[c, i, b, cz + 8 : cz + 9, :] = above[c, i, b : b + 1, :]

        @pl.when(exists(d))
        def _(i=i, d=d):
            for c in range(2):
                for b in range(nb):
                    g = below(c, i, b, slice(7, 8), cr[DESCENTS, d - 4, 1 - c, b : b + 1, :])
                    pot[c, i, b, 7:8, :] = pot[c, i, b, 8:9, :] + g

    def finish(i):
        for c in range(3):
            for b in range(nb):
                out_r[c, i - 2, :, lanes(b)] = fld[c, i, b, core, :] + mu * fb2[c, i, b, core, :]

    for s in range(DESCENTS):
        left_sums(s)
    fric_copy.wait()
    drag = jnp.zeros((cz, LANES), f32)
    for k in range(cz):
        drag = jnp.where(row_core == k, fric[k], drag)
    z_at = gz * cz + row_rim - 1
    z_in = (z_at >= 0) & (z_at < gzn * cz)

    def induced_plane(dst, i, acc):
        mid, dx, dy, dz = differ(pot, (0, 1, 2), i, 7, rim, lane_rim)
        x_at = gx * cx + i - 2
        factor = jnp.where(z_in & ((x_at >= 0) & (x_at < gxn * cx)), 0.5, 0.0)
        rows = pl.ds(7, rim)
        for b in range(nb):
            dst[0, i, b, rows, :] = factor * (dy(2, b) - dz(1, b))
            dst[1, i, b, rows, :] = factor * (dz(0, b) - dx(2, b))
            dst[2, i, b, rows, :] = factor * (dx(1, b) - dy(0, b))
        return acc

    def relax_plane(i, acc):
        mid, dx, dy, dz = differ(eb, (0, 1, 2), i, 8, cz, lane_core)
        for b in range(nb):
            w = relaxing(mid, dx, dy, dz, drag, b)
            for c in range(3):
                pot[c, i, b, core, :] = pot[c, i, b, core, :] + w[c]
        return acc

    out_d[...] = drag
    for s in range(RELAX):
        r = DESCENTS + s
        last = s == RELAX - 1
        induced = functools.partial(induced_plane, out_e if last else eb)
        if s == 0:
            lax.fori_loop(1, cx + 3, induced, 0, unroll=3)
        else:
            inner_planes(r, pot, None, induced, 0, 2)
            take_x(r, pot, pot, None)
            over_edges(induced, 0, 1, 2, 4)
        if last:
            break

        def relax(i, acc):
            acc = relax_plane(i, acc)
            pack_plane(r + 1, i, pot)
            return acc

        over_edges(relax, 0, 2, 2, 4)
        send_x(r + 1, pot)
        pack_corners(r + 1, pot)
        send_corners(r + 1)
        later_planes(r + 1, relax, 0)
        loop(2, cx + 2, finish)
        for slot in range(2):
            columns(False, lambda k, part: column_copy(slot, k, part, False).wait_send())


def finish_kernel(cx, cz, nb, rel, pot, induced, drag_ref, out_r, out_p, buf, sem, rsem):
    lane = lax.broadcasted_iota(jnp.int32, (cz, LANES), 1)
    drag = drag_ref[...]
    rel_copy = pltpu.make_async_copy(rel, out_r, rsem)
    rel_copy.start()
    step = math.gcd(cx, 4)

    def copy(k):
        planes = pl.ds(k * step, step)
        return pltpu.make_async_copy(buf.at[:, planes], out_p.at[:, planes], sem.at[k])

    def some(k, _):
        for j in range(step):
            i = k * step + j
            mid, dx, dy, dz = differ(induced, (0, 1, 2), i + 2, 8, cz, lane)
            for b in range(nb):
                w = relaxing(mid, dx, dy, dz, drag, b)
                for c in range(3):
                    buf[c, i, :, b * LANES : (b + 1) * LANES] = pot[c, i + 2, b, 8 : 8 + cz, :] + w[c]
        copy(k).start()
        return 0

    lax.fori_loop(0, cx // step, some, 0)
    for k in range(cx // step):
        copy(k).wait()
    rel_copy.wait()


def body(magnetic, friction):
    _, cx, cz, ny = magnetic.shape
    gxn, gzn = lax.axis_size("gx"), lax.axis_size("gz")
    nb = ny // LANES
    n = gxn * gzn
    full = (cx + 4, nb, cz + 16, LANES)
    VM = lambda *shape: pltpu.VMEM(shape, jnp.float32)
    DMA = lambda *shape: pltpu.SemaphoreType.DMA(shape)
    like = lambda *shape: jax.ShapeDtypeStruct(shape, jnp.float32)
    shape = like(*magnetic.shape)
    inner = pl.BlockSpec(memory_space=pltpu.VMEM)
    outer = pl.BlockSpec(memory_space=pltpu.HBM)
    stay = lambda x: pltpu.with_memory_space_constraint(x, pltpu.HBM)
    limit = 40 * 1024 * 1024
    relaxed, pot, induced, drag = pl.pallas_call(
        functools.partial(kernel, gxn, gzn, cx, cz, nb),
        out_shape=(shape, like(3, *full), like(3, *full), like(cz, LANES)),
        in_specs=[outer, outer],
        out_specs=(inner, inner, inner, inner),
        scratch_shapes=[
            VM(3, *full), VM(3, *full), VM(3, *full), VM(4, *full),
            pltpu.SMEM((cz,), jnp.float32),
            VM(ROUNDS, 2, 3, 2, nb, cz, LANES),
            VM(ROUNDS, 2, 3, cx, 2 * nb, LANES), VM(ROUNDS, 2, 3, cx, 2 * nb, LANES),
            VM(ROUNDS, 4, 3, nb, LANES), VM(ROUNDS, 4, 3, nb, LANES),
            VM(DESCENTS, 2, LANES), VM(DESCENTS, n, 2, LANES),
            VM(2, 2, cx, nb, LANES), VM(2, gzn, 2, cx + 4, nb, LANES), VM(2, cx + 4, nb, LANES),
            DMA(2, 2, 2), DMA(ROUNDS, 2, 2), DMA(2, 2, 2), DMA(ROUNDS, 2, 2),
            DMA(2, 8), DMA(ROUNDS, 8),
            DMA(DESCENTS), DMA(DESCENTS), DMA(2, gzn - 1, 3), DMA(2, gzn - 1, 3), DMA(nb + 1),
            pltpu.SemaphoreType.REGULAR((2,)),
        ],
        compiler_params=pltpu.CompilerParams(
            collective_id=0, has_side_effects=True, vmem_limit_bytes=limit
        ),
    )(stay(magnetic), stay(friction))
    return pl.pallas_call(
        functools.partial(finish_kernel, cx, cz, nb),
        out_shape=(shape, shape),
        in_specs=[inner] * 4,
        out_specs=(outer, outer),
        scratch_shapes=[VM(*magnetic.shape), DMA(cx // math.gcd(cx, 4)), pltpu.SemaphoreType.DMA],
        compiler_params=pltpu.CompilerParams(vmem_limit_bytes=limit),
    )(relaxed, pot, induced, drag)


def solution(mesh):
    return jax.shard_map(
        body,
        mesh=mesh,
        in_specs=(P(None, "gx", "gz", "runs"), P("gz")),
        out_specs=(P(None, "gx", "gz", "runs"), P(None, "gx", "gz", "runs")),
        check_vma=False,
    )
```

```python
import functools
import math

import jax
import jax.numpy as jnp
from jax import lax
from jax.experimental import pallas as pl
from jax.experimental.pallas import tpu as pltpu
from jax.sharding import PartitionSpec as P

DESCENTS = 2
RELAX = 2
ROUNDS = 1 + (DESCENTS - 1) + RELAX
LANES = 128

step_scale = 0.5
time_step = 0.2

DIRS = ((-1, 0), (1, 0), (0, -1), (0, 1), (-1, -1), (-1, 1), (1, -1), (1, 1))
PARTS = ((((0, 3, True),),) * DESCENTS + (((1, 2, True), (0, 1, False)),) + (((1, 3, True), (0, 1, False)),) * (RELAX - 1))
ZCOMPS = (3,) * DESCENTS + (2,) + (3,) * (RELAX - 1)
OPP = (1, 0, 3, 2, 7, 6, 5, 4)


def cross(l, r):
    return [l[1] * r[2] - l[2] * r[1], l[2] * r[0] - l[0] * r[2], l[0] * r[1] - l[1] * r[0]]


def dot(l, r):
    return l[0] * r[0] + l[1] * r[1] + l[2] * r[2]


def place(rows, columns, back):
    natural, kept = (1, 0) if back else (0, 1)
    y = lax.broadcasted_iota(jnp.int32, (rows, columns), natural)
    j = lax.broadcasted_iota(jnp.int32, (rows, columns), kept)
    nb = columns // LANES
    return jnp.where(y == nb * (j % LANES) + j // LANES, 1.0, 0.0).astype(jnp.bfloat16)


def split(x, parts):
    rows = x.shape[0]
    high = x.astype(jnp.bfloat16)
    parts[0:rows, :] = high
    parts[rows : 2 * rows, :] = (x - high.astype(jnp.float32)).astype(jnp.bfloat16)


def joined(parts, order):
    rows = parts.shape[0] // 2
    y = jnp.dot(parts[...], order[...], preferred_element_type=jnp.float32)
    return y[:rows] + y[rows:]


def moved(x, parts, order):
    split(x, parts)
    return joined(parts, order)


def differ(ref, comps, i, r0, rows):
    nb = ref.shape[2]
    mid = {c: [ref[c, i, b, pl.ds(r0, rows), :] for b in range(nb)] for c in comps}

    def dy(c, b):
        up = mid[c][b + 1] if b < nb - 1 else pltpu.roll(mid[c][0], LANES - 1, 1)
        down = mid[c][b - 1] if b else pltpu.roll(mid[c][nb - 1], 1, 1)
        return up - down

    def dx(c, b):
        return ref[c, i + 1, b, pl.ds(r0, rows), :] - ref[c, i - 1, b, pl.ds(r0, rows), :]

    def dz(c, b):
        return ref[c, i, b, pl.ds(r0 + 1, rows), :] - ref[c, i, b, pl.ds(r0 - 1, rows), :]

    return mid, dx, dy, dz


def relaxing(mid, dx, dy, dz, drag, b):
    B = [mid[c][b] for c in range(3)]
    J = [dy(2, b) - dz(1, b), dz(0, b) - dx(2, b), dx(1, b) - dy(0, b)]
    inv = (0.5 * time_step) / (drag * jnp.maximum(dot(B, B), 1.0))
    v = [u * inv for u in cross(J, B)]
    return cross(v, B)


def kernel(
    gxn, gzn, cx, cz, nb, mag, friction, out_r, pot, out_e, out_d, back,
    fld, fb, fb2, eb, fric, stage, parts, order, xr, zs, zr, cs, cr, ps, pr, ts, tr, above,
    xsend, xrecv, zsend, zrecv, ssem, rsem, psend, precv, tsend, trecv, insem, far,
):
    gx = lax.axis_index("gx")
    gz = lax.axis_index("gz")
    n = gxn * gzn
    me = gz * gxn + gx
    core = pl.ds(8, cz)
    f32 = jnp.float32

    def in_copy(c):
        return pltpu.make_async_copy(mag.at[c], stage.at[c], insem.at[c])

    for c in range(3):
        in_copy(c).start()
    fric_copy = pltpu.make_async_copy(friction, fric, insem.at[3])
    fric_copy.start()

    barrier = pltpu.get_barrier_semaphore()

    def peer(j):
        other = (me + j) % n
        return {"gz": other // gxn, "gx": other % gxn}

    def exists(d):
        dx, dz = DIRS[d]
        tests = []
        if dx:
            tests.append(gx > 0 if dx < 0 else gx < gxn - 1)
        if dz:
            tests.append(gz > 0 if dz < 0 else gz < gzn - 1)
        return functools.reduce(jnp.logical_and, tests)

    around = sum(jnp.where(exists(d), 1, 0) for d in range(8))

    def greet(sem):
        for d, (dx, dz) in enumerate(DIRS):
            @pl.when(exists(d))
            def _(dx=dx, dz=dz):
                pl.semaphore_signal(
                    sem, inc=1, device_id={"gz": gz + dz, "gx": gx + dx}, device_id_type=pl.DeviceIdType.MESH
                )

    greet(barrier)

    waves = max(gxn, gzn) - 2

    def wave_send(p):
        if p < waves:
            greet(far.at[p % 2])

    def wave_take(p):
        if p < waves:
            pl.semaphore_wait(far.at[p % 2], around)

    for ref in (fld, pot):
        for c in range(3):
            for i in (0, 1, cx + 2, cx + 3):
                ref[c, i] = jnp.zeros(ref.shape[2:], f32)

        def clear(i, _):
            for c in range(3):
                for b in range(nb):
                    ref[c, i, b, 0:8, :] = jnp.zeros((8, LANES), f32)
                    ref[c, i, b, cz + 8 : cz + 16, :] = jnp.zeros((8, LANES), f32)
            return 0

        lax.fori_loop(2, cx + 2, clear, 0)

    tr[...] = jnp.zeros(tr.shape, f32)
    order[...] = place(*order.shape, False)
    back[...] = place(*back.shape, True)

    def arrange(c, _):
        in_copy(c).wait()
        x = moved(stage[c].reshape(cx * cz, nb * LANES), parts, order)
        for i in range(cx):
            for b in range(nb):
                fld[c, i + 2, b, core, :] = x[i * cz : (i + 1) * cz, b * LANES : (b + 1) * LANES]
        return 0

    lax.fori_loop(0, 3, arrange, 0)

    def near(side):
        return 1 if side == 0 else 0

    def x_link(r, d, q, src, arriving):
        c0, c1, both = PARTS[r][q]
        slot = d if arriving else OPP[d]
        start = (2 if d == 0 else cx) + (0 if both else near(OPP[d]))
        first, count = (0, 2) if both else (near(slot), 1)
        return pltpu.make_async_remote_copy(
            src_ref=src.at[pl.ds(c0, c1 - c0), pl.ds(start, count), :, core, :],
            dst_ref=xr.at[r, slot, pl.ds(c0, c1 - c0), pl.ds(first, count)],
            send_sem=xsend.at[r % 2, d, q], recv_sem=xrecv.at[r, slot, q],
            device_id={"gz": gz, "gx": gx + DIRS[d][0]}, device_id_type=pl.DeviceIdType.MESH,
        )

    half = cx // 2

    def z_link(r, d, h, arriving):
        o = d if arriving else OPP[d]
        comps, planes = pl.ds(0, ZCOMPS[r]), pl.ds(h * half, half)
        return pltpu.make_async_remote_copy(
            src_ref=zs.at[r, d - 2, comps, planes], dst_ref=zr.at[r, o - 2, comps, planes],
            send_sem=zsend.at[r % 2, d - 2, h], recv_sem=zrecv.at[r, o - 2, h],
            device_id={"gz": gz + DIRS[d][1], "gx": gx}, device_id_type=pl.DeviceIdType.MESH,
        )

    def link(r, d, arriving):
        dx, dz = DIRS[d]
        o = d if arriving else OPP[d]
        return pltpu.make_async_remote_copy(
            src_ref=cs.at[r, d - 4], dst_ref=cr.at[r, o - 4], send_sem=ssem.at[r % 2, d], recv_sem=rsem.at[r, o],
            device_id={"gz": gz + dz, "gx": gx + dx}, device_id_type=pl.DeviceIdType.MESH,
        )

    def send_x(r, src):
        for d in (0, 1):
            @pl.when(exists(d))
            def _(d=d):
                for q in range(len(PARTS[r])):
                    x_link(r, d, q, src, False).start()

    def pack_plane(r, i, src):
        for c in range(ZCOMPS[r]):
            for b in range(nb):
                zs[r, 0, c, i - 2, 2 * b : 2 * b + 2, :] = src[c, i, b, 8:10, :]
                zs[r, 1, c, i - 2, 2 * b : 2 * b + 2, :] = src[c, i, b, cz + 6 : cz + 8, :]

    def pack_corners(r, src):
        for d in range(4, 8):
            dx, dz = DIRS[d]
            i = 2 if dx < 0 else cx + 1
            k = 8 if dz < 0 else cz + 7
            for c in range(3):
                for b in range(nb):
                    cs[r, d - 4, c, b : b + 1, :] = src[c, i, b, k : k + 1, :]

    def send_corners(r):
        for d in range(4, 8):
            @pl.when(exists(d))
            def _(d=d):
                link(r, d, False).start()

    def send_z(r, h):
        for d in (2, 3):
            @pl.when(exists(d))
            def _(d=d):
                z_link(r, d, h, False).start()

    def loop(low, high, do, unroll=1):
        def step(i, _):
            do(i)
            return 0

        lax.fori_loop(low, high, step, 0, unroll=unroll)

    def put(old, new, mu):
        return new if mu is None else old + mu * new

    def take_z(r, dst, mu, h):
        for d in (2, 3):
            @pl.when(exists(d))
            def _(d=d):
                z_link(r, d, h, True).wait_recv()
                row = 6 if d == 2 else cz + 8

                def unpack(i):
                    for c in range(ZCOMPS[r]):
                        for b in range(nb):
                            dst[c, i + 2, b, row : row + 2, :] = put(
                                dst[c, i + 2, b, row : row + 2, :], zr[r, d - 2, c, i, 2 * b : 2 * b + 2, :], mu
                            )

                loop(h * half, h * half + half, unpack, 2)
                z_link(r, d, h, False).wait_send()

    def inner_planes(r, dst, mu, do, acc, unroll=1):
        acc = lax.fori_loop(3, cx + 1, lambda i, acc: do(i, acc, inner_tiles), acc, unroll=2)
        for h in range(2):
            take_z(r, dst, mu, h)
            low, high = (3, half + 1) if h == 0 else (half + 1, cx + 1)
            acc = lax.fori_loop(low, high, lambda i, acc: do(i, acc, outer_tiles), acc, unroll=unroll)
        return acc

    def later_planes(r, do, acc, unroll=3):
        acc = lax.fori_loop(4, half + 2, do, acc, unroll=unroll)
        send_z(r, 0)
        acc = lax.fori_loop(half + 2, cx, do, acc, unroll=unroll)
        send_z(r, 1)
        return acc

    def take_x(r, src, dst, mu):
        for d in (4, 5, 6, 7):
            dx, dz = DIRS[d]

            @pl.when(exists(d))
            def _(d=d, dx=dx, dz=dz):
                link(r, d, True).wait_recv()
                i = 1 if dx < 0 else cx + 2
                k = 7 if dz < 0 else cz + 8
                if dst is not None:
                    for c in range(3):
                        for b in range(nb):
                            dst[c, i, b, k : k + 1, :] = put(
                                dst[c, i, b, k : k + 1, :], cr[r, d - 4, c, b : b + 1, :], mu
                            )
                link(r, d, False).wait_send()

        for d in (0, 1):
            @pl.when(exists(d))
            def _(d=d):
                base = 0 if d == 0 else cx + 2
                for q, (c0, c1, both) in enumerate(PARTS[r]):
                    x_link(r, d, q, src, True).wait_recv()
                    if dst is None:
                        continue
                    for c in range(c0, c1):
                        for p in range(2) if both else (near(d),):
                            for b in range(nb):
                                dst[c, base + p, b, core, :] = put(
                                    dst[c, base + p, b, core, :], xr[r, d, c, p, b], mu
                                )

        for d in (0, 1):
            @pl.when(exists(d))
            def _(d=d):
                for q in range(len(PARTS[r])):
                    x_link(r, d, q, src, False).wait_send()

    def over_edges(do, acc, low, width, unroll=1):
        def step(j, acc):
            return do(low + j + jnp.where(j >= width, cx + 3 - 2 * low - 2 * width + 1, 0), acc)

        return lax.fori_loop(0, 2 * width, step, acc, unroll=unroll)

    def folded(v):
        total = v[0:8]
        for k in range(8, v.shape[0], 8):
            total = total + v[k : k + 8]
        return total

    row_core = lax.broadcasted_iota(jnp.int32, (cz, LANES), 0)

    row = lax.broadcasted_iota(jnp.int32, (8, LANES), 0)
    last_tile = cz // 8
    inner_tiles, outer_tiles = tuple(range(1, last_tile)), (0, last_tile)
    all_tiles = tuple(range(last_tile + 1))

    def omega_plane(i, acc, tiles=all_tiles):
        here = (i >= 2) & (i < cx + 2)
        for t in tiles:
            mid, dx, dy, dz = differ(fld, (0, 1, 2), i, 7 + 8 * t, 8)
            rows = pl.ds(7 + 8 * t, 8)
            total = None
            for b in range(nb):
                B = [mid[c][b] for c in range(3)]
                J = [
                    0.5 * (dy(2, b) - dz(1, b)),
                    0.5 * (dz(0, b) - dx(2, b)),
                    0.5 * (dx(1, b) - dy(0, b)),
                ]
                D = 0.5 * (dx(0, b) + dy(1, b) + dz(2, b))
                square = dot(B, B)
                inv = 1.0 / jnp.maximum(square, 1.0)
                part = square * inv
                L = cross(J, B)
                Li = [u * inv for u in L]
                E = cross(Li, B)
                for c in range(3):
                    eb[c, i, b, rows, :] = E[c]
                eb[3, i, b, rows, :] = D * part
                drive = dot(L, Li)
                dd = D * D
                scale = inv * (drive + (dd * part - dd))
                lj = cross(Li, J)
                for c in range(3):
                    fb[c, i, b, rows, :] = scale * B[c] - lj[c]
                total = drive + dd if total is None else total + (drive + dd)
            inside = here
            if t == 0:
                inside = here & (row >= 1)
            elif t == last_tile:
                inside = here & (row == 0)
            acc = acc + jnp.where(inside, total, 0.0)
        return acc

    def force_plane(i, acc):
        mid, dx, dy, dz = differ(eb, (0, 1, 2, 3), i, 8, cz)
        for b in range(nb):
            curl = [
                dy(2, b) - dz(1, b) + dx(3, b),
                dz(0, b) - dx(2, b) + dy(3, b),
                dx(1, b) - dy(0, b) + dz(3, b),
            ]
            F = [fb[c, i, b, core, :] + 0.5 * curl[c] for c in range(3)]
            for c in range(3):
                fb2[c, i, b, core, :] = F[c]
            acc = acc + folded(dot(F, F))
        return acc

    def psum_copy(s, slot, j):
        return pltpu.make_async_remote_copy(
            src_ref=ps.at[s], dst_ref=pr.at[s, slot], send_sem=psend.at[s], recv_sem=precv.at[s],
            device_id=peer(j), device_id_type=pl.DeviceIdType.MESH,
        )

    def send_sums(s, lsum, gsum):
        ps[s, 0:1, :] = jnp.sum(lsum, axis=0, keepdims=True)
        ps[s, 1:2, :] = jnp.sum(gsum, axis=0, keepdims=True)

        def go(j, _):
            psum_copy(s, me, j).start()
            return 0

        lax.fori_loop(1, n, go, 0, unroll=3)

    def take_sums(s):
        pr[s, me] = ps[s]
        others = pr.at[s, pl.ds(0, n - 1)]
        pltpu.make_async_copy(others, others, precv.at[s]).wait()
        total = functools.reduce(lambda t, k: t + pr[s, k], range(1, n), pr[s, 0])
        sums = jnp.sum(total, axis=1, keepdims=True) / (n * cx * cz * nb * LANES)
        return step_scale * sums[0:1] / (sums[1:2] + 1e-6)

    def left_sums(s):
        others = pr.at[s, pl.ds(0, n - 1)]
        pltpu.make_async_copy(others, others, psend.at[s]).wait()

    def suffix_plane(i, src, dst):
        for c, other, sign in ((0, 1, -1.0), (1, 0, 1.0)):
            for b in range(nb):
                v = sign * src[other, i, b, core, :]
                step = 1
                while step < cz:
                    v = v + jnp.where(row_core < cz - step, pltpu.roll(v, cz - step, 0), 0.0)
                    step *= 2
                dst[c, i, b, core, :] = v

    def column_plane(i, src, slot):
        for c in range(2):
            for b in range(nb):
                ts[slot, c, i - 2, b : b + 1, :] = src[c, i, b, 8:9, :]

    GROUPS = (pl.ds(0, 2), pl.ds(2, 1))
    SIDES = ((0, 0, cx, 2), (1, 0, 2, cx + 2), (-1, cx - 2, 2, 0))

    def column_copy(group, part, arriving):
        dx, first, count, land = SIDES[part]
        dx, dz = (dx, 1) if arriving else (-dx, -1)
        return pltpu.make_async_remote_copy(
            src_ref=ts.at[GROUPS[group], :, pl.ds(first, count)],
            dst_ref=tr.at[GROUPS[group], :, pl.ds(land, count)],
            send_sem=tsend.at[group, part], recv_sem=trecv.at[group, part],
            device_id={"gz": gz + dz, "gx": gx + dx}, device_id_type=pl.DeviceIdType.MESH,
        )

    def columns(parts, arriving, do):
        for part in parts:
            dx = SIDES[part][0] if arriving else -SIDES[part][0]
            test = gz < gzn - 1 if arriving else gz > 0
            if dx:
                test = jnp.logical_and(test, gx > 0 if dx < 0 else gx < gxn - 1)

            @pl.when(test)
            def _(part=part):
                do(part)

    def send_columns(group):
        columns((0, 1, 2), False, lambda part: column_copy(group, part, False).start())

    def add_columns(group):
        column_copy(group, 0, True).wait_recv()

        def one(i):
            for slot in (0, 1) if group == 0 else (2,):
                for c in range(2):
                    ts[slot, c, i] = ts[slot, c, i] + tr[slot, c, i + 2]

        loop(0, cx, one, 2)
        send_columns(group)

    def first_columns(group):
        @pl.when(gz == gzn - 1)
        def _():
            send_columns(group)

    def pass_columns(group, low=0, high=gzn - 1):
        for k in range(high - 1, low - 1, -1):
            @pl.when(gz == k)
            def _():
                add_columns(group)

    loop(2, cx + 2, lambda i: pack_plane(0, i, fld), 2)
    pack_corners(0, fld)
    pl.semaphore_wait(barrier, around)
    send_x(0, fld)
    send_z(0, 0)
    send_z(0, 1)
    send_corners(0)
    wave_send(0)

    def first_suffix(i):
        suffix_plane(i, fld, pot)
        column_plane(i, pot, 0)

    loop(2, cx + 2, first_suffix, 2)
    zero = jnp.zeros((8, LANES), f32)
    mu = None
    for s in range(DESCENTS):
        last = s == DESCENTS - 1
        lsum = inner_planes(s, fld, mu, omega_plane, zero)
        if s == 0:
            wave_take(0)
            wave_send(1)
        take_x(s, fld if s == 0 else fb2, fld, mu)
        if s == 1:
            pass_columns(0, gzn - 2)
        lsum = over_edges(omega_plane, lsum, 1, 2)

        def suffix(i):
            held = fb if last else out_e
            suffix_plane(i, fb2, held)
            column_plane(i, held, s + 1)

        def force(i, acc):
            acc = force_plane(i, acc)
            pack_plane(s + 1, i, fb2)
            if last:
                suffix(i)
            return acc

        gsum = over_edges(force, zero, 2, 2, 4)
        gsum = lax.fori_loop(4, cx, force, gsum, unroll=4)
        pack_corners(s + 1, fb2)
        if s == 0:
            for p in range(1, waves):
                wave_take(p)
                wave_send(p + 1)
        send_sums(s, lsum, gsum)
        if last:
            first_columns(1)
        send_z(s + 1, 0)
        send_z(s + 1, 1)
        send_x(s + 1, fb if last else fb2)
        send_corners(s + 1)
        if last:
            over_edges(lambda i, acc: (suffix_plane(i, fld, pot), acc)[1], 0, 0, 2, 2)

            def advance(i):
                for c in range(2):
                    for b in range(nb):
                        pot[c, i, b, core, :] = pot[c, i, b, core, :] + mu * out_e[c, i, b, core, :]
                for b in range(nb):
                    pot[2, i, b, core, :] = jnp.zeros((cz, LANES), f32)

            loop(2, cx + 2, advance, 2)
            pass_columns(0, 0, gzn - 2)
            fric_copy.wait()
            drag = jnp.zeros((cz, LANES), f32)
            for k in range(cz):
                drag = jnp.where(row_core == k, fric[k], drag)
            out_d[...] = drag
            pass_columns(1)
            columns((1, 2), True, lambda part: column_copy(0, part, True).wait_recv())

            def older(i):
                for c in range(2):
                    above[c, i] = tr[0, c, i] + mu * tr[1, c, i]

            loop(0, cx + 4, older, 2)
            columns((1, 2), True, lambda part: column_copy(1, part, True).wait_recv())
        else:
            loop(2, cx + 2, suffix, 2)
            first_columns(0)
        mu = take_sums(s)

        def update(i):
            for c in range(3):
                for b in range(nb):
                    fld[c, i, b, core, :] = fld[c, i, b, core, :] + mu * fb2[c, i, b, core, :]

        if not last:
            loop(2, cx + 2, update, 2)


    def newer(i):
        for c in range(2):
            above[c, i] = above[c, i] + mu * tr[2, c, i]

    loop(0, cx + 4, newer, 2)
    for s in range(DESCENTS):
        left_sums(s)
    drag = out_d[...]

    def induced_plane(dst, i, acc, tiles=all_tiles):
        x_at = gx * cx + i - 2
        x_in = (x_at >= 0) & (x_at < gxn * cx)
        for t in tiles:
            mid, dx, dy, dz = differ(pot, (0, 1, 2), i, 7 + 8 * t, 8)
            z_at = gz * cz + row - 1 + 8 * t
            factor = jnp.where((z_at >= 0) & (z_at < gzn * cz) & x_in, 0.5, 0.0)
            rows = pl.ds(7 + 8 * t, 8)
            for b in range(nb):
                dst[0, i, b, rows, :] = factor * (dy(2, b) - dz(1, b))
                dst[1, i, b, rows, :] = factor * (dz(0, b) - dx(2, b))
                dst[2, i, b, rows, :] = factor * (dx(1, b) - dy(0, b))
        return acc

    def relax_plane(i, acc):
        mid, dx, dy, dz = differ(eb, (0, 1, 2), i, 8, cz)
        for b in range(nb):
            w = relaxing(mid, dx, dy, dz, drag, b)
            for c in range(3):
                pot[c, i, b, core, :] = pot[c, i, b, core, :] + w[c]
        return acc

    def lift(i):
        for c in range(2):
            for b in range(nb):
                pot[c, i, b, core, :] = (pot[c, i, b, core, :] + mu * fb[c, i, b, core, :]) + above[c, i, b : b + 1, :]

    loop(2, cx + 2, lift, 2)
    early = functools.partial(induced_plane, eb)
    lax.fori_loop(3, cx + 1, lambda i, acc: early(i, acc, inner_tiles), 0, unroll=2)
    take_x(DESCENTS, fb, None, None)
    for d in (0, 1):
        @pl.when(exists(d))
        def _(d=d):
            base = 0 if d == 0 else cx + 2
            for c, p in ((0, near(d)), (1, 0), (1, 1)):
                i = base + p
                for b in range(nb):
                    pot[c, i, b, core, :] = (
                        pot[c, i, b, core, :] + mu * xr[DESCENTS, d, c, p, b]
                    ) + above[c, i, b : b + 1, :]

    def below(c, i, b, rows, force):
        return (1.0 if c else -1.0) * (fld[1 - c, i, b, rows, :] + mu * force)

    for h in range(2):
        @pl.when(exists(2))
        def _(h=h):
            z_link(DESCENTS, 2, h, True).wait_recv()

            def low_rows(i):
                for c in range(2):
                    for b in range(nb):
                        g = below(c, i + 2, b, slice(6, 8), zr[DESCENTS, 0, 1 - c, i, 2 * b : 2 * b + 2, :])
                        row = pot[c, i + 2, b, 8:9, :] + g[1:2]
                        pot[c, i + 2, b, 7:8, :] = row
                        pot[c, i + 2, b, 6:7, :] = row + g[0:1]

            loop(h * half, h * half + half, low_rows)
            z_link(DESCENTS, 2, h, False).wait_send()

        @pl.when(exists(3))
        def _(h=h):
            z_link(DESCENTS, 3, h, True).wait_recv()

            def high_rows(i):
                for c in range(2):
                    for b in range(nb):
                        g = below(
                            c, i + 2, b, slice(cz + 8, cz + 9), zr[DESCENTS, 1, 1 - c, i, 2 * b : 2 * b + 1, :]
                        )
                        row = above[c, i + 2, b : b + 1, :]
                        pot[c, i + 2, b, cz + 8 : cz + 9, :] = row
                        pot[c, i + 2, b, cz + 9 : cz + 10, :] = row - g

            loop(h * half, h * half + half, high_rows)
            z_link(DESCENTS, 3, h, False).wait_send()

    for i, d in ((1, 4), (cx + 2, 6)):
        for c in range(2):
            for b in range(nb):
                pot[c, i, b, cz + 8 : cz + 9, :] = above[c, i, b : b + 1, :]

        @pl.when(exists(d))
        def _(i=i, d=d):
            for c in range(2):
                for b in range(nb):
                    g = below(c, i, b, slice(7, 8), cr[DESCENTS, d - 4, 1 - c, b : b + 1, :])
                    pot[c, i, b, 7:8, :] = pot[c, i, b, 8:9, :] + g

    def finish(c, _):
        for i in range(cx):
            for b in range(nb):
                stage[c, i, :, b * LANES : (b + 1) * LANES] = (
                    fld[c, i + 2, b, core, :] + mu * fb2[c, i + 2, b, core, :]
                )
        out_r[c] = moved(stage[c].reshape(cx * cz, nb * LANES), parts, back).reshape(cx, cz, nb * LANES)
        return 0

    for s in range(RELAX):
        r = DESCENTS + s
        last = s == RELAX - 1
        induced = functools.partial(induced_plane, out_e if last else eb)
        if s:
            inner_planes(r, pot, None, induced, 0, 2)
            take_x(r, pot, pot, None)
            over_edges(induced, 0, 1, 2, 4)
        if last:
            break

        def relax(i, acc):
            acc = relax_plane(i, acc)
            pack_plane(r + 1, i, pot)
            return acc

        over_edges(induced, 0, 1, 2, 4)
        over_edges(lambda i, acc: induced(i, acc, outer_tiles), 0, 3, 2, 4)
        over_edges(relax, 0, 2, 2, 4)
        send_x(r + 1, pot)
        pack_corners(r + 1, pot)
        send_corners(r + 1)
        lax.fori_loop(5, cx - 1, lambda i, acc: induced(i, acc, outer_tiles), 0, unroll=2)
        later_planes(r + 1, relax, 0)
        lax.fori_loop(0, 3, finish, 0)
        for slot in range(2):
            columns((0, 1, 2), False, lambda part: column_copy(slot, part, False).wait_send())


def finish_kernel(cx, cz, nb, rel, pot, induced, drag_ref, back, out_r, out_p, buf, raw, parts, sem, rsem):
    drag = drag_ref[...]
    rel_copy = pltpu.make_async_copy(rel, out_r, rsem)
    rel_copy.start()
    step = math.gcd(cx, 4)

    count = cx // step
    rows = 3 * step * cz

    def copy(k):
        planes = pl.ds(k * step, step)
        return pltpu.make_async_copy(buf.at[:, planes], out_p.at[:, planes], sem.at[k])

    def relax(k):
        for j in range(step):
            i = k * step + j
            mid, dx, dy, dz = differ(induced, (0, 1, 2), i + 2, 8, cz)
            for b in range(nb):
                w = relaxing(mid, dx, dy, dz, drag, b)
                for c in range(3):
                    raw[k % 2, c, j, :, b * LANES : (b + 1) * LANES] = pot[c, i + 2, b, 8 : 8 + cz, :] + w[c]

    def write(k):
        x = moved(raw[k % 2].reshape(rows, nb * LANES), parts.at[k % 2], back)
        buf[:, k * step : (k + 1) * step] = x.reshape(3, step, cz, nb * LANES)
        copy(k).start()

    for k in range(count):
        relax(k)
        if k:
            write(k - 1)
    write(count - 1)
    for k in range(count):
        copy(k).wait()
    rel_copy.wait()


def body(magnetic, friction):
    _, cx, cz, ny = magnetic.shape
    gxn, gzn = lax.axis_size("gx"), lax.axis_size("gz")
    nb = ny // LANES
    n = gxn * gzn
    full = (cx + 4, nb, cz + 16, LANES)
    VM = lambda *shape: pltpu.VMEM(shape, jnp.float32)
    DMA = lambda *shape: pltpu.SemaphoreType.DMA(shape)
    like = lambda *shape: jax.ShapeDtypeStruct(shape, jnp.float32)
    shape = like(*magnetic.shape)
    inner = pl.BlockSpec(memory_space=pltpu.VMEM)
    outer = pl.BlockSpec(memory_space=pltpu.HBM)
    stay = lambda x: pltpu.with_memory_space_constraint(x, pltpu.HBM)
    step = math.gcd(cx, 4)
    limit = 40 * 1024 * 1024
    half = lambda rows: pltpu.VMEM((rows, ny), jnp.bfloat16)
    turn = jax.ShapeDtypeStruct((ny, ny), jnp.bfloat16)
    relaxed, pot, induced, drag, back = pl.pallas_call(
        functools.partial(kernel, gxn, gzn, cx, cz, nb),
        out_shape=(shape, like(3, *full), like(3, *full), like(cz, LANES), turn),
        in_specs=[outer, outer],
        out_specs=(inner,) * 5,
        scratch_shapes=[
            VM(3, *full), VM(3, *full), VM(3, *full), VM(4, *full),
            pltpu.SMEM((cz,), jnp.float32),
            VM(*magnetic.shape), half(2 * cx * cz), half(ny),
            VM(ROUNDS, 2, 3, 2, nb, cz, LANES),
            VM(ROUNDS, 2, 3, cx, 2 * nb, LANES), VM(ROUNDS, 2, 3, cx, 2 * nb, LANES),
            VM(ROUNDS, 4, 3, nb, LANES), VM(ROUNDS, 4, 3, nb, LANES),
            VM(DESCENTS, 2, LANES), VM(DESCENTS, n, 2, LANES),
            VM(3, 2, cx, nb, LANES), VM(3, 2, cx + 4, nb, LANES), VM(2, cx + 4, nb, LANES),
            DMA(2, 2, 2), DMA(ROUNDS, 2, 2), DMA(2, 2, 2), DMA(ROUNDS, 2, 2),
            DMA(2, 8), DMA(ROUNDS, 8),
            DMA(DESCENTS), DMA(DESCENTS), DMA(2, 3), DMA(2, 3), DMA(4),
            pltpu.SemaphoreType.REGULAR((2,)),
        ],
        compiler_params=pltpu.CompilerParams(
            collective_id=0, has_side_effects=True, vmem_limit_bytes=limit
        ),
    )(stay(magnetic), stay(friction))
    return pl.pallas_call(
        functools.partial(finish_kernel, cx, cz, nb),
        out_shape=(shape, shape),
        in_specs=[inner] * 5,
        out_specs=(outer, outer),
        scratch_shapes=[
            VM(*magnetic.shape), VM(2, 3, step, cz, ny), pltpu.VMEM((2, 6 * step * cz, ny), jnp.bfloat16),
            DMA(cx // step), pltpu.SemaphoreType.DMA,
        ],
        compiler_params=pltpu.CompilerParams(vmem_limit_bytes=limit),
    )(relaxed, pot, induced, drag, back)


def solution(mesh):
    return jax.shard_map(
        body,
        mesh=mesh,
        in_specs=(P(None, "gx", "gz", "runs"), P("gz")),
        out_specs=(P(None, "gx", "gz", "runs"), P(None, "gx", "gz", "runs")),
        check_vma=False,
    )
```

```python
import functools
import math

import jax
import jax.numpy as jnp
from jax import lax
from jax.experimental import pallas as pl
from jax.experimental.pallas import tpu as pltpu
from jax.sharding import PartitionSpec as P

DESCENTS = 2
RELAX = 2
ROUNDS = 1 + (DESCENTS - 1) + RELAX
LANES = 128

step_scale = 0.5
time_step = 0.2

DIRS = ((-1, 0), (1, 0), (0, -1), (0, 1), (-1, -1), (-1, 1), (1, -1), (1, 1))
PARTS = ((((0, 3, True),),) * DESCENTS + (((1, 2, True), (0, 1, False)),) + (((1, 3, True), (0, 1, False)),) * (RELAX - 1))
ZCOMPS = (3,) * DESCENTS + (2,) + (3,) * (RELAX - 1)
OPP = (1, 0, 3, 2, 7, 6, 5, 4)


def cross(l, r):
    return [l[1] * r[2] - l[2] * r[1], l[2] * r[0] - l[0] * r[2], l[0] * r[1] - l[1] * r[0]]


def dot(l, r):
    return l[0] * r[0] + l[1] * r[1] + l[2] * r[2]


def place(rows, columns, back):
    natural, kept = (1, 0) if back else (0, 1)
    y = lax.broadcasted_iota(jnp.int32, (rows, columns), natural)
    j = lax.broadcasted_iota(jnp.int32, (rows, columns), kept)
    nb = columns // LANES
    return jnp.where(y == nb * (j % LANES) + j // LANES, 1.0, 0.0).astype(jnp.bfloat16)


def split(x, parts):
    rows = x.shape[0]
    high = x.astype(jnp.bfloat16)
    parts[0:rows, :] = high
    parts[rows : 2 * rows, :] = (x - high.astype(jnp.float32)).astype(jnp.bfloat16)


def joined(parts, order):
    rows = parts.shape[0] // 2
    y = jnp.dot(parts[...], order[...], preferred_element_type=jnp.float32)
    return y[:rows] + y[rows:]


def moved(x, parts, order):
    split(x, parts)
    return joined(parts, order)


def differ(ref, comps, i, r0, rows):
    nb = ref.shape[2]
    mid = {c: [ref[c, i, b, pl.ds(r0, rows), :] for b in range(nb)] for c in comps}

    def dy(c, b):
        up = mid[c][b + 1] if b < nb - 1 else pltpu.roll(mid[c][0], LANES - 1, 1)
        down = mid[c][b - 1] if b else pltpu.roll(mid[c][nb - 1], 1, 1)
        return up - down

    def dx(c, b):
        return ref[c, i + 1, b, pl.ds(r0, rows), :] - ref[c, i - 1, b, pl.ds(r0, rows), :]

    def dz(c, b):
        return ref[c, i, b, pl.ds(r0 + 1, rows), :] - ref[c, i, b, pl.ds(r0 - 1, rows), :]

    return mid, dx, dy, dz


def relaxing(mid, dx, dy, dz, drag, b):
    B = [mid[c][b] for c in range(3)]
    J = [dy(2, b) - dz(1, b), dz(0, b) - dx(2, b), dx(1, b) - dy(0, b)]
    inv = (0.5 * time_step) / (drag * jnp.maximum(dot(B, B), 1.0))
    v = [u * inv for u in cross(J, B)]
    return cross(v, B)


def kernel(
    gxn, gzn, cx, cz, nb, mag, friction, out_r, pot, out_e, out_d, back,
    fld, fb, fb2, eb, fric, stage, parts, order, xr, zs, zr, cs, cr, ps, pr, ts, tr, above,
    xsend, xrecv, zsend, zrecv, ssem, rsem, psend, precv, tsend, trecv, insem, far,
):
    gx = lax.axis_index("gx")
    gz = lax.axis_index("gz")
    n = gxn * gzn
    me = gz * gxn + gx
    core = pl.ds(8, cz)
    f32 = jnp.float32

    def in_copy(c):
        return pltpu.make_async_copy(mag.at[c], stage.at[c], insem.at[c])

    for c in range(3):
        in_copy(c).start()
    fric_copy = pltpu.make_async_copy(friction, fric, insem.at[3])
    fric_copy.start()

    barrier = pltpu.get_barrier_semaphore()

    def peer(j):
        other = (me + j) % n
        return {"gz": other // gxn, "gx": other % gxn}

    def exists(d):
        dx, dz = DIRS[d]
        tests = []
        if dx:
            tests.append(gx > 0 if dx < 0 else gx < gxn - 1)
        if dz:
            tests.append(gz > 0 if dz < 0 else gz < gzn - 1)
        return functools.reduce(jnp.logical_and, tests)

    around = sum(jnp.where(exists(d), 1, 0) for d in range(8))

    def greet(sem):
        for d, (dx, dz) in enumerate(DIRS):
            @pl.when(exists(d))
            def _(dx=dx, dz=dz):
                pl.semaphore_signal(
                    sem, inc=1, device_id={"gz": gz + dz, "gx": gx + dx}, device_id_type=pl.DeviceIdType.MESH
                )

    greet(barrier)

    waves = max(gxn, gzn) - 2

    def wave_send(p):
        if p < waves:
            greet(far.at[p % 2])

    def wave_take(p):
        if p < waves:
            pl.semaphore_wait(far.at[p % 2], around)

    for ref in (fld, pot):
        for c in range(3):
            for i in (0, 1, cx + 2, cx + 3):
                ref[c, i] = jnp.zeros(ref.shape[2:], f32)

        def clear(i, _):
            for c in range(3):
                for b in range(nb):
                    ref[c, i, b, 0:8, :] = jnp.zeros((8, LANES), f32)
                    ref[c, i, b, cz + 8 : cz + 16, :] = jnp.zeros((8, LANES), f32)
            return 0

        lax.fori_loop(2, cx + 2, clear, 0)

    tr[...] = jnp.zeros(tr.shape, f32)
    order[...] = place(*order.shape, False)
    back[...] = place(*back.shape, True)

    def arrange(c, _):
        in_copy(c).wait()
        x = moved(stage[c].reshape(cx * cz, nb * LANES), parts, order)
        for i in range(cx):
            for b in range(nb):
                fld[c, i + 2, b, core, :] = x[i * cz : (i + 1) * cz, b * LANES : (b + 1) * LANES]
        return 0

    lax.fori_loop(0, 3, arrange, 0)

    def near(side):
        return 1 if side == 0 else 0

    def x_link(r, d, q, src, arriving):
        c0, c1, both = PARTS[r][q]
        slot = d if arriving else OPP[d]
        start = (2 if d == 0 else cx) + (0 if both else near(OPP[d]))
        first, count = (0, 2) if both else (near(slot), 1)
        return pltpu.make_async_remote_copy(
            src_ref=src.at[pl.ds(c0, c1 - c0), pl.ds(start, count), :, core, :],
            dst_ref=xr.at[r, slot, pl.ds(c0, c1 - c0), pl.ds(first, count)],
            send_sem=xsend.at[r % 2, d, q], recv_sem=xrecv.at[r, slot, q],
            device_id={"gz": gz, "gx": gx + DIRS[d][0]}, device_id_type=pl.DeviceIdType.MESH,
        )

    half = cx // 2

    def z_link(r, d, h, arriving):
        o = d if arriving else OPP[d]
        comps, planes = pl.ds(0, ZCOMPS[r]), pl.ds(h * half, half)
        return pltpu.make_async_remote_copy(
            src_ref=zs.at[r, d - 2, comps, planes], dst_ref=zr.at[r, o - 2, comps, planes],
            send_sem=zsend.at[r % 2, d - 2, h], recv_sem=zrecv.at[r, o - 2, h],
            device_id={"gz": gz + DIRS[d][1], "gx": gx}, device_id_type=pl.DeviceIdType.MESH,
        )

    def link(r, d, arriving):
        dx, dz = DIRS[d]
        o = d if arriving else OPP[d]
        return pltpu.make_async_remote_copy(
            src_ref=cs.at[r, d - 4], dst_ref=cr.at[r, o - 4], send_sem=ssem.at[r % 2, d - 4], recv_sem=rsem.at[r, o - 4],
            device_id={"gz": gz + dz, "gx": gx + dx}, device_id_type=pl.DeviceIdType.MESH,
        )

    def send_x(r, src):
        for d in (0, 1):
            @pl.when(exists(d))
            def _(d=d):
                for q in range(len(PARTS[r])):
                    x_link(r, d, q, src, False).start()

    def pack_plane(r, i, src):
        for c in range(ZCOMPS[r]):
            for b in range(nb):
                zs[r, 0, c, i - 2, 2 * b : 2 * b + 2, :] = src[c, i, b, 8:10, :]
                zs[r, 1, c, i - 2, 2 * b : 2 * b + 2, :] = src[c, i, b, cz + 6 : cz + 8, :]

    def pack_corners(r, src):
        for d in range(4, 8):
            dx, dz = DIRS[d]
            i = 2 if dx < 0 else cx + 1
            k = 8 if dz < 0 else cz + 7
            for c in range(3):
                for b in range(nb):
                    cs[r, d - 4, c, b : b + 1, :] = src[c, i, b, k : k + 1, :]

    def send_corners(r):
        for d in range(4, 8):
            @pl.when(exists(d))
            def _(d=d):
                link(r, d, False).start()

    def send_z(r, h):
        for d in (2, 3):
            @pl.when(exists(d))
            def _(d=d):
                z_link(r, d, h, False).start()

    def loop(low, high, do, unroll=1):
        def step(i, _):
            do(i)
            return 0

        lax.fori_loop(low, high, step, 0, unroll=unroll)

    def put(old, new, mu):
        return new if mu is None else old + mu * new

    def take_z(r, dst, mu, h):
        for d in (2, 3):
            @pl.when(exists(d))
            def _(d=d):
                z_link(r, d, h, True).wait_recv()
                row = 6 if d == 2 else cz + 8

                def unpack(i):
                    for c in range(ZCOMPS[r]):
                        for b in range(nb):
                            dst[c, i + 2, b, row : row + 2, :] = put(
                                dst[c, i + 2, b, row : row + 2, :], zr[r, d - 2, c, i, 2 * b : 2 * b + 2, :], mu
                            )

                loop(h * half, h * half + half, unpack, 2)
                z_link(r, d, h, False).wait_send()

    def inner_planes(r, dst, mu, do, acc, unroll=1):
        acc = lax.fori_loop(3, cx + 1, lambda i, acc: do(i, acc, inner_tiles), acc, unroll=2)
        for h in range(2):
            take_z(r, dst, mu, h)
            low, high = (3, half + 1) if h == 0 else (half + 1, cx + 1)
            acc = lax.fori_loop(low, high, lambda i, acc: do(i, acc, outer_tiles), acc, unroll=unroll)
        return acc

    def later_planes(r, do, acc, unroll=3):
        acc = lax.fori_loop(4, half + 2, do, acc, unroll=unroll)
        send_z(r, 0)
        acc = lax.fori_loop(half + 2, cx, do, acc, unroll=unroll)
        send_z(r, 1)
        return acc

    def take_x(r, src, dst, mu):
        for d in (4, 5, 6, 7):
            dx, dz = DIRS[d]

            @pl.when(exists(d))
            def _(d=d, dx=dx, dz=dz):
                link(r, d, True).wait_recv()
                i = 1 if dx < 0 else cx + 2
                k = 7 if dz < 0 else cz + 8
                if dst is not None:
                    for c in range(3):
                        for b in range(nb):
                            dst[c, i, b, k : k + 1, :] = put(
                                dst[c, i, b, k : k + 1, :], cr[r, d - 4, c, b : b + 1, :], mu
                            )
                link(r, d, False).wait_send()

        for d in (0, 1):
            @pl.when(exists(d))
            def _(d=d):
                base = 0 if d == 0 else cx + 2
                for q, (c0, c1, both) in enumerate(PARTS[r]):
                    x_link(r, d, q, src, True).wait_recv()
                    if dst is None:
                        continue
                    for c in range(c0, c1):
                        for p in range(2) if both else (near(d),):
                            for b in range(nb):
                                dst[c, base + p, b, core, :] = put(
                                    dst[c, base + p, b, core, :], xr[r, d, c, p, b], mu
                                )

        for d in (0, 1):
            @pl.when(exists(d))
            def _(d=d):
                for q in range(len(PARTS[r])):
                    x_link(r, d, q, src, False).wait_send()

    def over_edges(do, acc, low, width, unroll=1):
        def step(j, acc):
            return do(low + j + jnp.where(j >= width, cx + 3 - 2 * low - 2 * width + 1, 0), acc)

        return lax.fori_loop(0, 2 * width, step, acc, unroll=unroll)

    def folded(v):
        total = v[0:8]
        for k in range(8, v.shape[0], 8):
            total = total + v[k : k + 8]
        return total

    row_core = lax.broadcasted_iota(jnp.int32, (cz, LANES), 0)

    row = lax.broadcasted_iota(jnp.int32, (8, LANES), 0)
    last_tile = cz // 8
    inner_tiles, outer_tiles = tuple(range(1, last_tile)), (0, last_tile)
    all_tiles = tuple(range(last_tile + 1))

    def omega_plane(i, acc, tiles=all_tiles):
        here = (i >= 2) & (i < cx + 2)
        for t in tiles:
            mid, dx, dy, dz = differ(fld, (0, 1, 2), i, 7 + 8 * t, 8)
            rows = pl.ds(7 + 8 * t, 8)
            total = None
            for b in range(nb):
                B = [mid[c][b] for c in range(3)]
                J = [
                    0.5 * (dy(2, b) - dz(1, b)),
                    0.5 * (dz(0, b) - dx(2, b)),
                    0.5 * (dx(1, b) - dy(0, b)),
                ]
                D = 0.5 * (dx(0, b) + dy(1, b) + dz(2, b))
                square = dot(B, B)
                inv = 1.0 / jnp.maximum(square, 1.0)
                part = square * inv
                L = cross(J, B)
                Li = [u * inv for u in L]
                E = cross(Li, B)
                for c in range(3):
                    eb[c, i, b, rows, :] = E[c]
                eb[3, i, b, rows, :] = D * part
                drive = dot(L, Li)
                dd = D * D
                scale = inv * (drive + (dd * part - dd))
                lj = cross(Li, J)
                for c in range(3):
                    fb[c, i, b, rows, :] = scale * B[c] - lj[c]
                total = drive + dd if total is None else total + (drive + dd)
            inside = here
            if t == 0:
                inside = here & (row >= 1)
            elif t == last_tile:
                inside = here & (row == 0)
            acc = acc + jnp.where(inside, total, 0.0)
        return acc

    def force_plane(i, acc):
        mid, dx, dy, dz = differ(eb, (0, 1, 2, 3), i, 8, cz)
        for b in range(nb):
            curl = [
                dy(2, b) - dz(1, b) + dx(3, b),
                dz(0, b) - dx(2, b) + dy(3, b),
                dx(1, b) - dy(0, b) + dz(3, b),
            ]
            F = [fb[c, i, b, core, :] + 0.5 * curl[c] for c in range(3)]
            for c in range(3):
                fb2[c, i, b, core, :] = F[c]
            acc = acc + folded(dot(F, F))
        return acc

    def psum_copy(s, slot, j):
        return pltpu.make_async_remote_copy(
            src_ref=ps.at[s], dst_ref=pr.at[s, slot], send_sem=psend.at[s], recv_sem=precv.at[s],
            device_id=peer(j), device_id_type=pl.DeviceIdType.MESH,
        )

    def send_sums(s, lsum, gsum):
        ps[s, 0:1, :] = jnp.sum(lsum, axis=0, keepdims=True)
        ps[s, 1:2, :] = jnp.sum(gsum, axis=0, keepdims=True)

        def go(j, _):
            psum_copy(s, me, j).start()
            return 0

        lax.fori_loop(1, n, go, 0, unroll=3)

    def take_sums(s):
        pr[s, me] = ps[s]
        others = pr.at[s, pl.ds(0, n - 1)]
        pltpu.make_async_copy(others, others, precv.at[s]).wait()
        total = functools.reduce(lambda t, k: t + pr[s, k], range(1, n), pr[s, 0])
        sums = jnp.sum(total, axis=1, keepdims=True) / (n * cx * cz * nb * LANES)
        return step_scale * sums[0:1] / (sums[1:2] + 1e-6)

    def left_sums(s):
        others = pr.at[s, pl.ds(0, n - 1)]
        pltpu.make_async_copy(others, others, psend.at[s]).wait()

    def suffix_plane(i, src, dst):
        for c, other, sign in ((0, 1, -1.0), (1, 0, 1.0)):
            for b in range(nb):
                v = sign * src[other, i, b, core, :]
                step = 1
                while step < cz:
                    v = v + jnp.where(row_core < cz - step, pltpu.roll(v, cz - step, 0), 0.0)
                    step *= 2
                dst[c, i, b, core, :] = v

    def column_plane(i, src, slot):
        for c in range(2):
            for b in range(nb):
                ts[slot, c, i - 2, b : b + 1, :] = src[c, i, b, 8:9, :]

    GROUPS = (pl.ds(0, 2), pl.ds(2, 1))
    SIDES = ((0, 0, cx, 2), (1, 0, 2, cx + 2), (-1, cx - 2, 2, 0))

    def column_copy(group, part, arriving):
        dx, first, count, land = SIDES[part]
        dx, dz = (dx, 1) if arriving else (-dx, -1)
        return pltpu.make_async_remote_copy(
            src_ref=ts.at[GROUPS[group], :, pl.ds(first, count)],
            dst_ref=tr.at[GROUPS[group], :, pl.ds(land, count)],
            send_sem=tsend.at[group, part], recv_sem=trecv.at[group, part],
            device_id={"gz": gz + dz, "gx": gx + dx}, device_id_type=pl.DeviceIdType.MESH,
        )

    def columns(parts, arriving, do):
        for part in parts:
            dx = SIDES[part][0] if arriving else -SIDES[part][0]
            test = gz < gzn - 1 if arriving else gz > 0
            if dx:
                test = jnp.logical_and(test, gx > 0 if dx < 0 else gx < gxn - 1)

            @pl.when(test)
            def _(part=part):
                do(part)

    def send_columns(group):
        columns((0, 1, 2), False, lambda part: column_copy(group, part, False).start())

    def add_columns(group):
        column_copy(group, 0, True).wait_recv()

        def one(i):
            for slot in (0, 1) if group == 0 else (2,):
                for c in range(2):
                    ts[slot, c, i] = ts[slot, c, i] + tr[slot, c, i + 2]

        loop(0, cx, one, 2)
        send_columns(group)

    def first_columns(group):
        @pl.when(gz == gzn - 1)
        def _():
            send_columns(group)

    def pass_columns(group, low=0, high=gzn - 1):
        if low < high:
            @pl.when((gz >= low) & (gz < high))
            def _():
                add_columns(group)

    loop(2, cx + 2, lambda i: pack_plane(0, i, fld), 2)
    pack_corners(0, fld)
    pl.semaphore_wait(barrier, around)
    send_x(0, fld)
    send_z(0, 0)
    send_z(0, 1)
    send_corners(0)
    wave_send(0)

    def first_suffix(i):
        suffix_plane(i, fld, pot)
        column_plane(i, pot, 0)

    loop(2, cx + 2, first_suffix, 2)
    zero = jnp.zeros((8, LANES), f32)
    mu = None
    for s in range(DESCENTS):
        last = s == DESCENTS - 1
        lsum = inner_planes(s, fld, mu, omega_plane, zero, 2)
        if s == 0:
            wave_take(0)
            wave_send(1)
        take_x(s, fld if s == 0 else fb2, fld, mu)
        if s == 1:
            pass_columns(0, max(gzn - 3, 0), gzn - 2)
        lsum = over_edges(omega_plane, lsum, 1, 2, 2)

        def suffix(i):
            held = fb if last else out_e
            suffix_plane(i, fb2, held)
            column_plane(i, held, s + 1)

        def force(i, acc):
            acc = force_plane(i, acc)
            pack_plane(s + 1, i, fb2)
            if last:
                suffix(i)
            return acc

        gsum = over_edges(force, zero, 2, 2, 4)
        gsum = lax.fori_loop(4, cx, force, gsum, unroll=4)
        pack_corners(s + 1, fb2)
        if s == 0:
            for p in range(1, waves):
                wave_take(p)
                wave_send(p + 1)
        send_sums(s, lsum, gsum)
        if last:
            first_columns(1)
        def send_rows(when):
            @pl.when(when)
            def _():
                send_z(s + 1, 0)
                send_z(s + 1, 1)

        second = gz == gzn - 2
        send_rows(jnp.logical_not(second) if last else gz >= 0)
        send_x(s + 1, fb if last else fb2)
        send_corners(s + 1)
        if last:
            over_edges(lambda i, acc: (suffix_plane(i, fld, pot), acc)[1], 0, 0, 2, 2)

            def advance(i):
                for c in range(2):
                    for b in range(nb):
                        pot[c, i, b, core, :] = pot[c, i, b, core, :] + mu * out_e[c, i, b, core, :]
                for b in range(nb):
                    pot[2, i, b, core, :] = jnp.zeros((cz, LANES), f32)

            loop(2, cx + 2, advance, 2)
            pass_columns(0, 0, gzn - 3)
            fric_copy.wait()
            drag = jnp.zeros((cz, LANES), f32)
            for k in range(cz):
                drag = jnp.where(row_core == k, fric[k], drag)
            out_d[...] = drag
            pass_columns(1)
            send_rows(second)
            columns((1, 2), True, lambda part: column_copy(0, part, True).wait_recv())

            def older(i):
                for c in range(2):
                    above[c, i] = tr[0, c, i] + mu * tr[1, c, i]

            loop(0, cx + 4, older, 2)
            columns((1, 2), True, lambda part: column_copy(1, part, True).wait_recv())
        else:
            loop(2, cx + 2, suffix, 2)
            first_columns(0)
            pass_columns(0, max(gzn - 2, 0), gzn - 1)
        mu = take_sums(s)

        def update(i):
            for c in range(3):
                for b in range(nb):
                    fld[c, i, b, core, :] = fld[c, i, b, core, :] + mu * fb2[c, i, b, core, :]

        if not last:
            loop(2, cx + 2, update, 2)


    def newer(i):
        for c in range(2):
            above[c, i] = above[c, i] + mu * tr[2, c, i]

    loop(0, cx + 4, newer, 2)
    for s in range(DESCENTS):
        left_sums(s)
    drag = out_d[...]

    def induced_plane(dst, i, acc, tiles=all_tiles):
        x_at = gx * cx + i - 2
        x_in = (x_at >= 0) & (x_at < gxn * cx)
        for t in tiles:
            mid, dx, dy, dz = differ(pot, (0, 1, 2), i, 7 + 8 * t, 8)
            z_at = gz * cz + row - 1 + 8 * t
            factor = jnp.where((z_at >= 0) & (z_at < gzn * cz) & x_in, 0.5, 0.0)
            rows = pl.ds(7 + 8 * t, 8)
            for b in range(nb):
                dst[0, i, b, rows, :] = factor * (dy(2, b) - dz(1, b))
                dst[1, i, b, rows, :] = factor * (dz(0, b) - dx(2, b))
                dst[2, i, b, rows, :] = factor * (dx(1, b) - dy(0, b))
        return acc

    def relax_plane(i, acc):
        mid, dx, dy, dz = differ(eb, (0, 1, 2), i, 8, cz)
        for b in range(nb):
            w = relaxing(mid, dx, dy, dz, drag, b)
            for c in range(3):
                pot[c, i, b, core, :] = pot[c, i, b, core, :] + w[c]
        return acc

    def lift(i):
        for c in range(2):
            for b in range(nb):
                pot[c, i, b, core, :] = (pot[c, i, b, core, :] + mu * fb[c, i, b, core, :]) + above[c, i, b : b + 1, :]

    loop(2, cx + 2, lift, 2)
    early = functools.partial(induced_plane, eb)
    lax.fori_loop(3, cx + 1, lambda i, acc: early(i, acc, inner_tiles), 0, unroll=2)
    take_x(DESCENTS, fb, None, None)
    for d in (0, 1):
        @pl.when(exists(d))
        def _(d=d):
            base = 0 if d == 0 else cx + 2
            for c, p in ((0, near(d)), (1, 0), (1, 1)):
                i = base + p
                for b in range(nb):
                    pot[c, i, b, core, :] = (
                        pot[c, i, b, core, :] + mu * xr[DESCENTS, d, c, p, b]
                    ) + above[c, i, b : b + 1, :]

    def below(c, i, b, rows, force):
        return (1.0 if c else -1.0) * (fld[1 - c, i, b, rows, :] + mu * force)

    for h in range(2):
        @pl.when(exists(2))
        def _(h=h):
            z_link(DESCENTS, 2, h, True).wait_recv()

            def low_rows(i):
                for c in range(2):
                    for b in range(nb):
                        g = below(c, i + 2, b, slice(6, 8), zr[DESCENTS, 0, 1 - c, i, 2 * b : 2 * b + 2, :])
                        row = pot[c, i + 2, b, 8:9, :] + g[1:2]
                        pot[c, i + 2, b, 7:8, :] = row
                        pot[c, i + 2, b, 6:7, :] = row + g[0:1]

            loop(h * half, h * half + half, low_rows)
            z_link(DESCENTS, 2, h, False).wait_send()

        @pl.when(exists(3))
        def _(h=h):
            z_link(DESCENTS, 3, h, True).wait_recv()

            def high_rows(i):
                for c in range(2):
                    for b in range(nb):
                        g = below(
                            c, i + 2, b, slice(cz + 8, cz + 9), zr[DESCENTS, 1, 1 - c, i, 2 * b : 2 * b + 1, :]
                        )
                        row = above[c, i + 2, b : b + 1, :]
                        pot[c, i + 2, b, cz + 8 : cz + 9, :] = row
                        pot[c, i + 2, b, cz + 9 : cz + 10, :] = row - g

            loop(h * half, h * half + half, high_rows)
            z_link(DESCENTS, 3, h, False).wait_send()

    for i, d in ((1, 4), (cx + 2, 6)):
        for c in range(2):
            for b in range(nb):
                pot[c, i, b, cz + 8 : cz + 9, :] = above[c, i, b : b + 1, :]

        @pl.when(exists(d))
        def _(i=i, d=d):
            for c in range(2):
                for b in range(nb):
                    g = below(c, i, b, slice(7, 8), cr[DESCENTS, d - 4, 1 - c, b : b + 1, :])
                    pot[c, i, b, 7:8, :] = pot[c, i, b, 8:9, :] + g

    def finish(c, _):
        for i in range(cx):
            for b in range(nb):
                stage[c, i, :, b * LANES : (b + 1) * LANES] = (
                    fld[c, i + 2, b, core, :] + mu * fb2[c, i + 2, b, core, :]
                )
        out_r[c] = moved(stage[c].reshape(cx * cz, nb * LANES), parts, back).reshape(cx, cz, nb * LANES)
        return 0

    for s in range(RELAX):
        r = DESCENTS + s
        last = s == RELAX - 1
        induced = functools.partial(induced_plane, out_e if last else eb)
        if s:
            inner_planes(r, pot, None, induced, 0, 2)
            take_x(r, pot, pot, None)
            over_edges(induced, 0, 1, 2, 4)
        if last:
            break

        def relax(i, acc):
            acc = relax_plane(i, acc)
            pack_plane(r + 1, i, pot)
            return acc

        over_edges(induced, 0, 1, 2, 4)
        over_edges(lambda i, acc: induced(i, acc, outer_tiles), 0, 3, 2, 4)
        over_edges(relax, 0, 2, 2, 4)
        send_x(r + 1, pot)
        pack_corners(r + 1, pot)
        send_corners(r + 1)
        lax.fori_loop(5, cx - 1, lambda i, acc: induced(i, acc, outer_tiles), 0, unroll=2)
        later_planes(r + 1, relax, 0)
        lax.fori_loop(0, 3, finish, 0)
        for slot in range(2):
            columns((0, 1, 2), False, lambda part: column_copy(slot, part, False).wait_send())


def finish_kernel(cx, cz, nb, rel, pot, induced, drag_ref, back, out_r, out_p, buf, raw, parts, sem, rsem):
    drag = drag_ref[...]
    rel_copy = pltpu.make_async_copy(rel, out_r, rsem)
    rel_copy.start()
    step = math.gcd(cx, 2)

    count = cx // step
    rows = 3 * step * cz

    def copy(k):
        planes = pl.ds(k * step, step)
        return pltpu.make_async_copy(buf.at[:, planes], out_p.at[:, planes], sem.at[k])

    def relax(k):
        for j in range(step):
            i = k * step + j
            mid, dx, dy, dz = differ(induced, (0, 1, 2), i + 2, 8, cz)
            for b in range(nb):
                w = relaxing(mid, dx, dy, dz, drag, b)
                for c in range(3):
                    raw[k % 2, c, j, :, b * LANES : (b + 1) * LANES] = pot[c, i + 2, b, 8 : 8 + cz, :] + w[c]

    def write(k):
        x = moved(raw[k % 2].reshape(rows, nb * LANES), parts.at[k % 2], back)
        buf[:, k * step : (k + 1) * step] = x.reshape(3, step, cz, nb * LANES)
        copy(k).start()

    for k in range(count):
        relax(k)
        if k:
            write(k - 1)
    write(count - 1)
    for k in range(count):
        copy(k).wait()
    rel_copy.wait()


def body(magnetic, friction):
    _, cx, cz, ny = magnetic.shape
    gxn, gzn = lax.axis_size("gx"), lax.axis_size("gz")
    nb = ny // LANES
    n = gxn * gzn
    full = (cx + 4, nb, cz + 16, LANES)
    VM = lambda *shape: pltpu.VMEM(shape, jnp.float32)
    DMA = lambda *shape: pltpu.SemaphoreType.DMA(shape)
    like = lambda *shape: jax.ShapeDtypeStruct(shape, jnp.float32)
    shape = like(*magnetic.shape)
    inner = pl.BlockSpec(memory_space=pltpu.VMEM)
    outer = pl.BlockSpec(memory_space=pltpu.HBM)
    stay = lambda x: pltpu.with_memory_space_constraint(x, pltpu.HBM)
    step = math.gcd(cx, 2)
    limit = 40 * 1024 * 1024
    half = lambda rows: pltpu.VMEM((rows, ny), jnp.bfloat16)
    turn = jax.ShapeDtypeStruct((ny, ny), jnp.bfloat16)
    relaxed, pot, induced, drag, back = pl.pallas_call(
        functools.partial(kernel, gxn, gzn, cx, cz, nb),
        out_shape=(shape, like(3, *full), like(3, *full), like(cz, LANES), turn),
        in_specs=[outer, outer],
        out_specs=(inner,) * 5,
        scratch_shapes=[
            VM(3, *full), VM(3, *full), VM(3, *full), VM(4, *full),
            pltpu.SMEM((cz,), jnp.float32),
            VM(*magnetic.shape), half(2 * cx * cz), half(ny),
            VM(ROUNDS, 2, 3, 2, nb, cz, LANES),
            VM(ROUNDS, 2, 3, cx, 2 * nb, LANES), VM(ROUNDS, 2, 3, cx, 2 * nb, LANES),
            VM(ROUNDS, 4, 3, nb, LANES), VM(ROUNDS, 4, 3, nb, LANES),
            VM(DESCENTS, 2, LANES), VM(DESCENTS, n, 2, LANES),
            VM(3, 2, cx, nb, LANES), VM(3, 2, cx + 4, nb, LANES), VM(2, cx + 4, nb, LANES),
            DMA(2, 2, 2), DMA(ROUNDS, 2, 2), DMA(2, 2, 2), DMA(ROUNDS, 2, 2),
            DMA(2, 4), DMA(ROUNDS, 4),
            DMA(DESCENTS), DMA(DESCENTS), DMA(2, 3), DMA(2, 3), DMA(4),
            pltpu.SemaphoreType.REGULAR((2,)),
        ],
        compiler_params=pltpu.CompilerParams(
            collective_id=0, has_side_effects=True, vmem_limit_bytes=limit
        ),
    )(stay(magnetic), stay(friction))
    return pl.pallas_call(
        functools.partial(finish_kernel, cx, cz, nb),
        out_shape=(shape, shape),
        in_specs=[inner] * 5,
        out_specs=(outer, outer),
        scratch_shapes=[
            VM(*magnetic.shape), VM(2, 3, step, cz, ny), pltpu.VMEM((2, 6 * step * cz, ny), jnp.bfloat16),
            DMA(cx // step), pltpu.SemaphoreType.DMA,
        ],
        compiler_params=pltpu.CompilerParams(vmem_limit_bytes=limit),
    )(relaxed, pot, induced, drag, back)


def solution(mesh):
    return jax.shard_map(
        body,
        mesh=mesh,
        in_specs=(P(None, "gx", "gz", "runs"), P("gz")),
        out_specs=(P(None, "gx", "gz", "runs"), P(None, "gx", "gz", "runs")),
        check_vma=False,
    )
```

```python
import functools
import math

import jax
import jax.numpy as jnp
from jax import lax
from jax.experimental import pallas as pl
from jax.experimental.pallas import tpu as pltpu
from jax.sharding import PartitionSpec as P

DESCENTS = 2
RELAX = 2
ROUNDS = 1 + (DESCENTS - 1) + RELAX
LANES = 128

step_scale = 0.5
time_step = 0.2

DIRS = ((-1, 0), (1, 0), (0, -1), (0, 1), (-1, -1), (-1, 1), (1, -1), (1, 1))
PARTS = ((((0, 3, True),),) * DESCENTS + (((1, 2, True), (0, 1, False)),) + (((1, 3, True), (0, 1, False)),) * (RELAX - 1))
ZCOMPS = (3,) * DESCENTS + (2,) + (3,) * (RELAX - 1)
OPP = (1, 0, 3, 2, 7, 6, 5, 4)


def cross(l, r):
    return [l[1] * r[2] - l[2] * r[1], l[2] * r[0] - l[0] * r[2], l[0] * r[1] - l[1] * r[0]]


def dot(l, r):
    return l[0] * r[0] + l[1] * r[1] + l[2] * r[2]


def place(rows, columns, back):
    natural, kept = (1, 0) if back else (0, 1)
    y = lax.broadcasted_iota(jnp.int32, (rows, columns), natural)
    j = lax.broadcasted_iota(jnp.int32, (rows, columns), kept)
    nb = columns // LANES
    return jnp.where(y == nb * (j % LANES) + j // LANES, 1.0, 0.0).astype(jnp.bfloat16)


def split(x, parts):
    rows = x.shape[0]
    high = x.astype(jnp.bfloat16)
    parts[0:rows, :] = high
    parts[rows : 2 * rows, :] = (x - high.astype(jnp.float32)).astype(jnp.bfloat16)


def joined(parts, order):
    rows = parts.shape[0] // 2
    y = jnp.dot(parts[...], order[...], preferred_element_type=jnp.float32)
    return y[:rows] + y[rows:]


def moved(x, parts, order):
    split(x, parts)
    return joined(parts, order)


def differ(ref, comps, i, r0, rows):
    nb = ref.shape[2]
    mid = {c: [ref[c, i, b, pl.ds(r0, rows), :] for b in range(nb)] for c in comps}

    def dy(c, b):
        up = mid[c][b + 1] if b < nb - 1 else pltpu.roll(mid[c][0], LANES - 1, 1)
        down = mid[c][b - 1] if b else pltpu.roll(mid[c][nb - 1], 1, 1)
        return up - down

    def dx(c, b):
        return ref[c, i + 1, b, pl.ds(r0, rows), :] - ref[c, i - 1, b, pl.ds(r0, rows), :]

    def dz(c, b):
        return ref[c, i, b, pl.ds(r0 + 1, rows), :] - ref[c, i, b, pl.ds(r0 - 1, rows), :]

    return mid, dx, dy, dz


def relaxing(mid, dx, dy, dz, drag, b):
    B = [mid[c][b] for c in range(3)]
    J = [dy(2, b) - dz(1, b), dz(0, b) - dx(2, b), dx(1, b) - dy(0, b)]
    inv = (0.5 * time_step) / (drag * jnp.maximum(dot(B, B), 1.0))
    v = [u * inv for u in cross(J, B)]
    return cross(v, B)


def kernel(
    gxn, gzn, cx, cz, nb, mag, friction, out_r, pot, out_e, out_d, back,
    fld, fb, fb2, eb, fric, stage, parts, order, xr, zs, zr, cs, cr, ps, pr, ts, tr, above,
    xsend, xrecv, zsend, zrecv, ssem, rsem, psend, precv, tsend, trecv, insem, far,
):
    gx = lax.axis_index("gx")
    gz = lax.axis_index("gz")
    n = gxn * gzn
    me = gz * gxn + gx
    core = pl.ds(8, cz)
    f32 = jnp.float32

    def in_copy(c):
        return pltpu.make_async_copy(mag.at[c], stage.at[c], insem.at[c])

    for c in range(3):
        in_copy(c).start()
    fric_copy = pltpu.make_async_copy(friction, fric, insem.at[3])
    fric_copy.start()

    barrier = pltpu.get_barrier_semaphore()

    def peer(j):
        other = (me + j) % n
        return {"gz": other // gxn, "gx": other % gxn}

    def exists(d):
        dx, dz = DIRS[d]
        tests = []
        if dx:
            tests.append(gx > 0 if dx < 0 else gx < gxn - 1)
        if dz:
            tests.append(gz > 0 if dz < 0 else gz < gzn - 1)
        return functools.reduce(jnp.logical_and, tests)

    around = sum(jnp.where(exists(d), 1, 0) for d in range(8))

    def greet(sem):
        for d, (dx, dz) in enumerate(DIRS):
            @pl.when(exists(d))
            def _(dx=dx, dz=dz):
                pl.semaphore_signal(
                    sem, inc=1, device_id={"gz": gz + dz, "gx": gx + dx}, device_id_type=pl.DeviceIdType.MESH
                )

    greet(barrier)

    waves = max(gxn, gzn) - 2

    def wave_send(p):
        if p < waves:
            greet(far.at[p % 2])

    def wave_take(p):
        if p < waves:
            pl.semaphore_wait(far.at[p % 2], around)

    for ref in (fld, pot):
        for c in range(3):
            for i in (0, 1, cx + 2, cx + 3):
                ref[c, i] = jnp.zeros(ref.shape[2:], f32)

        def clear(i, _):
            for c in range(3):
                for b in range(nb):
                    ref[c, i, b, 0:8, :] = jnp.zeros((8, LANES), f32)
                    ref[c, i, b, cz + 8 : cz + 16, :] = jnp.zeros((8, LANES), f32)
            return 0

        lax.fori_loop(2, cx + 2, clear, 0)

    tr[...] = jnp.zeros(tr.shape, f32)
    order[...] = place(*order.shape, False)
    back[...] = place(*back.shape, True)

    def arrange(c, _):
        in_copy(c).wait()
        x = moved(stage[c].reshape(cx * cz, nb * LANES), parts, order)
        for i in range(cx):
            for b in range(nb):
                fld[c, i + 2, b, core, :] = x[i * cz : (i + 1) * cz, b * LANES : (b + 1) * LANES]
        return 0

    lax.fori_loop(0, 3, arrange, 0)

    def near(side):
        return 1 if side == 0 else 0

    def x_link(r, d, q, src, arriving):
        c0, c1, both = PARTS[r][q]
        slot = d if arriving else OPP[d]
        start = (2 if d == 0 else cx) + (0 if both else near(OPP[d]))
        first, count = (0, 2) if both else (near(slot), 1)
        return pltpu.make_async_remote_copy(
            src_ref=src.at[pl.ds(c0, c1 - c0), pl.ds(start, count), :, core, :],
            dst_ref=xr.at[r, slot, pl.ds(c0, c1 - c0), pl.ds(first, count)],
            send_sem=xsend.at[r % 2, d, q], recv_sem=xrecv.at[r, slot, q],
            device_id={"gz": gz, "gx": gx + DIRS[d][0]}, device_id_type=pl.DeviceIdType.MESH,
        )

    half = cx // 2

    def z_link(r, d, h, arriving):
        o = d if arriving else OPP[d]
        comps, planes = pl.ds(0, ZCOMPS[r]), pl.ds(h * half, half)
        return pltpu.make_async_remote_copy(
            src_ref=zs.at[r, d - 2, comps, planes], dst_ref=zr.at[r, o - 2, comps, planes],
            send_sem=zsend.at[r % 2, d - 2, h], recv_sem=zrecv.at[r, o - 2, h],
            device_id={"gz": gz + DIRS[d][1], "gx": gx}, device_id_type=pl.DeviceIdType.MESH,
        )

    def link(r, d, arriving):
        dx, dz = DIRS[d]
        o = d if arriving else OPP[d]
        return pltpu.make_async_remote_copy(
            src_ref=cs.at[r, d - 4], dst_ref=cr.at[r, o - 4], send_sem=ssem.at[r % 2, d - 4], recv_sem=rsem.at[r, o - 4],
            device_id={"gz": gz + dz, "gx": gx + dx}, device_id_type=pl.DeviceIdType.MESH,
        )

    def send_x(r, src):
        for d in (0, 1):
            @pl.when(exists(d))
            def _(d=d):
                for q in range(len(PARTS[r])):
                    x_link(r, d, q, src, False).start()

    def pack_plane(r, i, src):
        for c in range(ZCOMPS[r]):
            for b in range(nb):
                zs[r, 0, c, i - 2, 2 * b : 2 * b + 2, :] = src[c, i, b, 8:10, :]
                zs[r, 1, c, i - 2, 2 * b : 2 * b + 2, :] = src[c, i, b, cz + 6 : cz + 8, :]

    def pack_corners(r, src):
        for d in range(4, 8):
            dx, dz = DIRS[d]
            i = 2 if dx < 0 else cx + 1
            k = 8 if dz < 0 else cz + 7
            for c in range(3):
                for b in range(nb):
                    cs[r, d - 4, c, b : b + 1, :] = src[c, i, b, k : k + 1, :]

    def send_corners(r):
        for d in range(4, 8):
            @pl.when(exists(d))
            def _(d=d):
                link(r, d, False).start()

    def send_z(r, h):
        for d in (2, 3):
            @pl.when(exists(d))
            def _(d=d):
                z_link(r, d, h, False).start()

    def loop(low, high, do, unroll=1):
        def step(i, _):
            do(i)
            return 0

        lax.fori_loop(low, high, step, 0, unroll=unroll)

    def put(old, new, mu):
        return new if mu is None else old + mu * new

    def take_z(r, dst, mu, h):
        for d in (2, 3):
            @pl.when(exists(d))
            def _(d=d):
                z_link(r, d, h, True).wait_recv()
                row = 6 if d == 2 else cz + 8

                def unpack(i):
                    for c in range(ZCOMPS[r]):
                        for b in range(nb):
                            dst[c, i + 2, b, row : row + 2, :] = put(
                                dst[c, i + 2, b, row : row + 2, :], zr[r, d - 2, c, i, 2 * b : 2 * b + 2, :], mu
                            )

                loop(h * half, h * half + half, unpack, 4)
                z_link(r, d, h, False).wait_send()

    def inner_planes(r, dst, mu, do, acc, unroll=1):
        acc = lax.fori_loop(3, cx + 1, lambda i, acc: do(i, acc, inner_tiles), acc, unroll=2)
        for h in range(2):
            take_z(r, dst, mu, h)
            low, high = (3, half + 1) if h == 0 else (half + 1, cx + 1)
            acc = lax.fori_loop(low, high, lambda i, acc: do(i, acc, outer_tiles), acc, unroll=unroll)
        return acc

    def later_planes(r, do, acc, unroll=3):
        acc = lax.fori_loop(4, half + 2, do, acc, unroll=unroll)
        send_z(r, 0)
        acc = lax.fori_loop(half + 2, cx, do, acc, unroll=unroll)
        send_z(r, 1)
        return acc

    def take_x(r, src, dst, mu):
        for d in (4, 5, 6, 7):
            dx, dz = DIRS[d]

            @pl.when(exists(d))
            def _(d=d, dx=dx, dz=dz):
                link(r, d, True).wait_recv()
                i = 1 if dx < 0 else cx + 2
                k = 7 if dz < 0 else cz + 8
                if dst is not None:
                    for c in range(3):
                        for b in range(nb):
                            dst[c, i, b, k : k + 1, :] = put(
                                dst[c, i, b, k : k + 1, :], cr[r, d - 4, c, b : b + 1, :], mu
                            )
                link(r, d, False).wait_send()

        for d in (0, 1):
            @pl.when(exists(d))
            def _(d=d):
                base = 0 if d == 0 else cx + 2
                for q, (c0, c1, both) in enumerate(PARTS[r]):
                    x_link(r, d, q, src, True).wait_recv()
                    if dst is None:
                        continue
                    for c in range(c0, c1):
                        for p in range(2) if both else (near(d),):
                            for b in range(nb):
                                dst[c, base + p, b, core, :] = put(
                                    dst[c, base + p, b, core, :], xr[r, d, c, p, b], mu
                                )

        for d in (0, 1):
            @pl.when(exists(d))
            def _(d=d):
                for q in range(len(PARTS[r])):
                    x_link(r, d, q, src, False).wait_send()

    def over_edges(do, acc, low, width, unroll=1):
        def step(j, acc):
            return do(low + j + jnp.where(j >= width, cx + 3 - 2 * low - 2 * width + 1, 0), acc)

        return lax.fori_loop(0, 2 * width, step, acc, unroll=unroll)

    def folded(v):
        total = v[0:8]
        for k in range(8, v.shape[0], 8):
            total = total + v[k : k + 8]
        return total

    row_core = lax.broadcasted_iota(jnp.int32, (cz, LANES), 0)

    row = lax.broadcasted_iota(jnp.int32, (8, LANES), 0)
    last_tile = cz // 8
    inner_tiles, outer_tiles = tuple(range(1, last_tile)), (0, last_tile)
    all_tiles = tuple(range(last_tile + 1))

    def omega_plane(i, acc, tiles=all_tiles):
        here = (i >= 2) & (i < cx + 2)
        for t in tiles:
            mid, dx, dy, dz = differ(fld, (0, 1, 2), i, 7 + 8 * t, 8)
            rows = pl.ds(7 + 8 * t, 8)
            total = None
            for b in range(nb):
                B = [mid[c][b] for c in range(3)]
                J = [
                    0.5 * (dy(2, b) - dz(1, b)),
                    0.5 * (dz(0, b) - dx(2, b)),
                    0.5 * (dx(1, b) - dy(0, b)),
                ]
                D = 0.5 * (dx(0, b) + dy(1, b) + dz(2, b))
                square = dot(B, B)
                inv = 1.0 / jnp.maximum(square, 1.0)
                part = square * inv
                L = cross(J, B)
                Li = [u * inv for u in L]
                E = cross(Li, B)
                for c in range(3):
                    eb[c, i, b, rows, :] = E[c]
                eb[3, i, b, rows, :] = D * part
                drive = dot(L, Li)
                dd = D * D
                scale = inv * (drive + (dd * part - dd))
                lj = cross(Li, J)
                for c in range(3):
                    fb[c, i, b, rows, :] = scale * B[c] - lj[c]
                total = drive + dd if total is None else total + (drive + dd)
            inside = here
            if t == 0:
                inside = here & (row >= 1)
            elif t == last_tile:
                inside = here & (row == 0)
            acc = acc + jnp.where(inside, total, 0.0)
        return acc

    def force_plane(i, acc):
        mid, dx, dy, dz = differ(eb, (0, 1, 2, 3), i, 8, cz)
        for b in range(nb):
            curl = [
                dy(2, b) - dz(1, b) + dx(3, b),
                dz(0, b) - dx(2, b) + dy(3, b),
                dx(1, b) - dy(0, b) + dz(3, b),
            ]
            F = [fb[c, i, b, core, :] + 0.5 * curl[c] for c in range(3)]
            for c in range(3):
                fb2[c, i, b, core, :] = F[c]
            acc = acc + folded(dot(F, F))
        return acc

    def psum_copy(s, slot, j):
        return pltpu.make_async_remote_copy(
            src_ref=ps.at[s], dst_ref=pr.at[s, slot], send_sem=psend.at[s], recv_sem=precv.at[s],
            device_id=peer(j), device_id_type=pl.DeviceIdType.MESH,
        )

    def send_sums(s, lsum, gsum):
        ps[s, 0:1, :] = jnp.sum(lsum, axis=0, keepdims=True)
        ps[s, 1:2, :] = jnp.sum(gsum, axis=0, keepdims=True)

        def go(j, _):
            psum_copy(s, me, j).start()
            return 0

        lax.fori_loop(1, n, go, 0, unroll=3)

    def take_sums(s):
        pr[s, me] = ps[s]
        others = pr.at[s, pl.ds(0, n - 1)]
        pltpu.make_async_copy(others, others, precv.at[s]).wait()
        total = functools.reduce(lambda t, k: t + pr[s, k], range(1, n), pr[s, 0])
        sums = jnp.sum(total, axis=1, keepdims=True) / (n * cx * cz * nb * LANES)
        return step_scale * sums[0:1] / (sums[1:2] + 1e-6)

    def left_sums(s):
        others = pr.at[s, pl.ds(0, n - 1)]
        pltpu.make_async_copy(others, others, psend.at[s]).wait()

    def suffix_plane(i, src, dst):
        for c, other, sign in ((0, 1, -1.0), (1, 0, 1.0)):
            for b in range(nb):
                v = sign * src[other, i, b, core, :]
                step = 1
                while step < cz:
                    v = v + jnp.where(row_core < cz - step, pltpu.roll(v, cz - step, 0), 0.0)
                    step *= 2
                dst[c, i, b, core, :] = v

    def column_plane(i, src, slot):
        for c in range(2):
            for b in range(nb):
                ts[slot, c, i - 2, b : b + 1, :] = src[c, i, b, 8:9, :]

    GROUPS = (pl.ds(0, 2), pl.ds(2, 1))
    SIDES = ((0, 0, cx, 2), (1, 0, 2, cx + 2), (-1, cx - 2, 2, 0))

    def column_copy(group, part, arriving):
        dx, first, count, land = SIDES[part]
        dx, dz = (dx, 1) if arriving else (-dx, -1)
        return pltpu.make_async_remote_copy(
            src_ref=ts.at[GROUPS[group], :, pl.ds(first, count)],
            dst_ref=tr.at[GROUPS[group], :, pl.ds(land, count)],
            send_sem=tsend.at[group, part], recv_sem=trecv.at[group, part],
            device_id={"gz": gz + dz, "gx": gx + dx}, device_id_type=pl.DeviceIdType.MESH,
        )

    def columns(parts, arriving, do):
        for part in parts:
            dx = SIDES[part][0] if arriving else -SIDES[part][0]
            test = gz < gzn - 1 if arriving else gz > 0
            if dx:
                test = jnp.logical_and(test, gx > 0 if dx < 0 else gx < gxn - 1)

            @pl.when(test)
            def _(part=part):
                do(part)

    def send_columns(group):
        columns((0, 1, 2), False, lambda part: column_copy(group, part, False).start())

    def add_columns(group):
        column_copy(group, 0, True).wait_recv()

        def one(i):
            for slot in (0, 1) if group == 0 else (2,):
                for c in range(2):
                    ts[slot, c, i] = ts[slot, c, i] + tr[slot, c, i + 2]

        loop(0, cx, one, 2)
        send_columns(group)

    def first_columns(group):
        @pl.when(gz == gzn - 1)
        def _():
            send_columns(group)

    def pass_columns(group, low=0, high=gzn - 1):
        if low < high:
            @pl.when((gz >= low) & (gz < high))
            def _():
                add_columns(group)

    loop(2, cx + 2, lambda i: pack_plane(0, i, fld), 2)
    pack_corners(0, fld)
    pl.semaphore_wait(barrier, around)
    send_x(0, fld)
    send_z(0, 0)
    send_z(0, 1)
    send_corners(0)
    wave_send(0)

    def first_suffix(i):
        suffix_plane(i, fld, pot)
        column_plane(i, pot, 0)

    loop(2, cx + 2, first_suffix, 2)
    zero = jnp.zeros((8, LANES), f32)
    mu = None
    for s in range(DESCENTS):
        last = s == DESCENTS - 1
        lsum = inner_planes(s, fld, mu, omega_plane, zero, 2)
        if s == 0:
            wave_take(0)
            wave_send(1)
        take_x(s, fld if s == 0 else fb2, fld, mu)
        if s == 1:
            pass_columns(0, max(gzn - 3, 0), gzn - 2)
        lsum = over_edges(omega_plane, lsum, 1, 2, 2)

        def suffix(i):
            held = fb if last else out_e
            suffix_plane(i, fb2, held)
            column_plane(i, held, s + 1)

        def force(i, acc):
            acc = force_plane(i, acc)
            pack_plane(s + 1, i, fb2)
            if last:
                suffix(i)
            return acc

        gsum = over_edges(force, zero, 2, 2, 4)
        gsum = lax.fori_loop(4, cx, force, gsum, unroll=4)
        pack_corners(s + 1, fb2)
        if s == 0:
            for p in range(1, waves):
                wave_take(p)
                wave_send(p + 1)
        send_sums(s, lsum, gsum)
        if last:
            first_columns(1)
        def send_rows(when):
            @pl.when(when)
            def _():
                send_z(s + 1, 0)
                send_z(s + 1, 1)

        second = gz == gzn - 2
        send_rows(jnp.logical_not(second) if last else gz >= 0)
        send_x(s + 1, fb if last else fb2)
        send_corners(s + 1)
        if last:
            over_edges(lambda i, acc: (suffix_plane(i, fld, pot), acc)[1], 0, 0, 2, 2)

            def advance(i):
                for c in range(2):
                    for b in range(nb):
                        pot[c, i, b, core, :] = pot[c, i, b, core, :] + mu * out_e[c, i, b, core, :]
                for b in range(nb):
                    pot[2, i, b, core, :] = jnp.zeros((cz, LANES), f32)

            loop(2, cx + 2, advance, 2)
            pass_columns(0, 0, gzn - 3)
            fric_copy.wait()
            drag = jnp.zeros((cz, LANES), f32)
            for k in range(cz):
                drag = jnp.where(row_core == k, fric[k], drag)
            out_d[...] = drag
            pass_columns(1)
            send_rows(second)
            columns((1, 2), True, lambda part: column_copy(0, part, True).wait_recv())

            def older(i):
                for c in range(2):
                    above[c, i] = tr[0, c, i] + mu * tr[1, c, i]

            loop(0, cx + 4, older, 2)
            columns((1, 2), True, lambda part: column_copy(1, part, True).wait_recv())
        else:
            loop(2, cx + 2, suffix, 2)
            first_columns(0)
            pass_columns(0, max(gzn - 2, 0), gzn - 1)
        mu = take_sums(s)

        def update(i):
            for c in range(3):
                for b in range(nb):
                    fld[c, i, b, core, :] = fld[c, i, b, core, :] + mu * fb2[c, i, b, core, :]

        if not last:
            loop(2, cx + 2, update, 4)


    def newer(i):
        for c in range(2):
            above[c, i] = above[c, i] + mu * tr[2, c, i]

    loop(0, cx + 4, newer, 2)
    for s in range(DESCENTS):
        left_sums(s)
    drag = out_d[...]

    def induced_plane(dst, i, acc, tiles=all_tiles):
        x_at = gx * cx + i - 2
        x_in = (x_at >= 0) & (x_at < gxn * cx)
        for t in tiles:
            mid, dx, dy, dz = differ(pot, (0, 1, 2), i, 7 + 8 * t, 8)
            z_at = gz * cz + row - 1 + 8 * t
            factor = jnp.where((z_at >= 0) & (z_at < gzn * cz) & x_in, 0.5, 0.0)
            rows = pl.ds(7 + 8 * t, 8)
            for b in range(nb):
                dst[0, i, b, rows, :] = factor * (dy(2, b) - dz(1, b))
                dst[1, i, b, rows, :] = factor * (dz(0, b) - dx(2, b))
                dst[2, i, b, rows, :] = factor * (dx(1, b) - dy(0, b))
        return acc

    def relax_plane(i, acc):
        mid, dx, dy, dz = differ(eb, (0, 1, 2), i, 8, cz)
        for b in range(nb):
            w = relaxing(mid, dx, dy, dz, drag, b)
            for c in range(3):
                pot[c, i, b, core, :] = pot[c, i, b, core, :] + w[c]
        return acc

    def lift(i):
        for c in range(2):
            for b in range(nb):
                pot[c, i, b, core, :] = (pot[c, i, b, core, :] + mu * fb[c, i, b, core, :]) + above[c, i, b : b + 1, :]

    loop(2, cx + 2, lift, 4)
    early = functools.partial(induced_plane, eb)
    lax.fori_loop(3, cx + 1, lambda i, acc: early(i, acc, inner_tiles), 0, unroll=2)
    take_x(DESCENTS, fb, None, None)
    for d in (0, 1):
        @pl.when(exists(d))
        def _(d=d):
            base = 0 if d == 0 else cx + 2
            for c, p in ((0, near(d)), (1, 0), (1, 1)):
                i = base + p
                for b in range(nb):
                    pot[c, i, b, core, :] = (
                        pot[c, i, b, core, :] + mu * xr[DESCENTS, d, c, p, b]
                    ) + above[c, i, b : b + 1, :]

    def below(c, i, b, rows, force):
        return (1.0 if c else -1.0) * (fld[1 - c, i, b, rows, :] + mu * force)

    for h in range(2):
        @pl.when(exists(2))
        def _(h=h):
            z_link(DESCENTS, 2, h, True).wait_recv()

            def low_rows(i):
                for c in range(2):
                    for b in range(nb):
                        g = below(c, i + 2, b, slice(6, 8), zr[DESCENTS, 0, 1 - c, i, 2 * b : 2 * b + 2, :])
                        row = pot[c, i + 2, b, 8:9, :] + g[1:2]
                        pot[c, i + 2, b, 7:8, :] = row
                        pot[c, i + 2, b, 6:7, :] = row + g[0:1]

            loop(h * half, h * half + half, low_rows, 4)
            z_link(DESCENTS, 2, h, False).wait_send()

        @pl.when(exists(3))
        def _(h=h):
            z_link(DESCENTS, 3, h, True).wait_recv()

            def high_rows(i):
                for c in range(2):
                    for b in range(nb):
                        g = below(
                            c, i + 2, b, slice(cz + 8, cz + 9), zr[DESCENTS, 1, 1 - c, i, 2 * b : 2 * b + 1, :]
                        )
                        row = above[c, i + 2, b : b + 1, :]
                        pot[c, i + 2, b, cz + 8 : cz + 9, :] = row
                        pot[c, i + 2, b, cz + 9 : cz + 10, :] = row - g

            loop(h * half, h * half + half, high_rows, 4)
            z_link(DESCENTS, 3, h, False).wait_send()

    for i, d in ((1, 4), (cx + 2, 6)):
        for c in range(2):
            for b in range(nb):
                pot[c, i, b, cz + 8 : cz + 9, :] = above[c, i, b : b + 1, :]

        @pl.when(exists(d))
        def _(i=i, d=d):
            for c in range(2):
                for b in range(nb):
                    g = below(c, i, b, slice(7, 8), cr[DESCENTS, d - 4, 1 - c, b : b + 1, :])
                    pot[c, i, b, 7:8, :] = pot[c, i, b, 8:9, :] + g

    def finish(c, _):
        for i in range(cx):
            for b in range(nb):
                stage[c, i, :, b * LANES : (b + 1) * LANES] = (
                    fld[c, i + 2, b, core, :] + mu * fb2[c, i + 2, b, core, :]
                )
        out_r[c] = moved(stage[c].reshape(cx * cz, nb * LANES), parts, back).reshape(cx, cz, nb * LANES)
        return 0

    for s in range(RELAX):
        r = DESCENTS + s
        last = s == RELAX - 1
        induced = functools.partial(induced_plane, out_e if last else eb)
        if s:
            inner_planes(r, pot, None, induced, 0, 2)
            take_x(r, pot, pot, None)
            over_edges(induced, 0, 1, 2, 4)
        if last:
            break

        def relax(i, acc):
            acc = relax_plane(i, acc)
            pack_plane(r + 1, i, pot)
            return acc

        over_edges(induced, 0, 1, 2, 4)
        over_edges(lambda i, acc: induced(i, acc, outer_tiles), 0, 3, 2, 4)
        over_edges(relax, 0, 2, 2, 4)
        send_x(r + 1, pot)
        pack_corners(r + 1, pot)
        send_corners(r + 1)
        lax.fori_loop(5, cx - 1, lambda i, acc: induced(i, acc, outer_tiles), 0, unroll=2)
        later_planes(r + 1, relax, 0)
        lax.fori_loop(0, 3, finish, 0)
        for slot in range(2):
            columns((0, 1, 2), False, lambda part: column_copy(slot, part, False).wait_send())


def finish_kernel(cx, cz, nb, rel, pot, induced, drag_ref, back, out_r, out_p, buf, raw, parts, sem, rsem):
    drag = drag_ref[...]
    rel_copy = pltpu.make_async_copy(rel, out_r, rsem)
    rel_copy.start()
    step = math.gcd(cx, 2)

    count = cx // step
    rows = 3 * step * cz

    def copy(k):
        planes = pl.ds(k * step, step)
        return pltpu.make_async_copy(buf.at[:, planes], out_p.at[:, planes], sem.at[k])

    def relax(k):
        for j in range(step):
            i = k * step + j
            mid, dx, dy, dz = differ(induced, (0, 1, 2), i + 2, 8, cz)
            for b in range(nb):
                w = relaxing(mid, dx, dy, dz, drag, b)
                for c in range(3):
                    raw[k % 2, c, j, :, b * LANES : (b + 1) * LANES] = pot[c, i + 2, b, 8 : 8 + cz, :] + w[c]

    def write(k):
        x = moved(raw[k % 2].reshape(rows, nb * LANES), parts.at[k % 2], back)
        buf[:, k * step : (k + 1) * step] = x.reshape(3, step, cz, nb * LANES)
        copy(k).start()

    for k in range(count):
        relax(k)
        if k:
            write(k - 1)
    write(count - 1)
    for k in range(count):
        copy(k).wait()
    rel_copy.wait()


def body(magnetic, friction):
    _, cx, cz, ny = magnetic.shape
    gxn, gzn = lax.axis_size("gx"), lax.axis_size("gz")
    nb = ny // LANES
    n = gxn * gzn
    full = (cx + 4, nb, cz + 16, LANES)
    VM = lambda *shape: pltpu.VMEM(shape, jnp.float32)
    DMA = lambda *shape: pltpu.SemaphoreType.DMA(shape)
    like = lambda *shape: jax.ShapeDtypeStruct(shape, jnp.float32)
    shape = like(*magnetic.shape)
    inner = pl.BlockSpec(memory_space=pltpu.VMEM)
    outer = pl.BlockSpec(memory_space=pltpu.HBM)
    stay = lambda x: pltpu.with_memory_space_constraint(x, pltpu.HBM)
    step = math.gcd(cx, 2)
    limit = 40 * 1024 * 1024
    half = lambda rows: pltpu.VMEM((rows, ny), jnp.bfloat16)
    turn = jax.ShapeDtypeStruct((ny, ny), jnp.bfloat16)
    relaxed, pot, induced, drag, back = pl.pallas_call(
        functools.partial(kernel, gxn, gzn, cx, cz, nb),
        out_shape=(shape, like(3, *full), like(3, *full), like(cz, LANES), turn),
        in_specs=[outer, outer],
        out_specs=(inner,) * 5,
        scratch_shapes=[
            VM(3, *full), VM(3, *full), VM(3, *full), VM(4, *full),
            pltpu.SMEM((cz,), jnp.float32),
            VM(*magnetic.shape), half(2 * cx * cz), half(ny),
            VM(ROUNDS, 2, 3, 2, nb, cz, LANES),
            VM(ROUNDS, 2, 3, cx, 2 * nb, LANES), VM(ROUNDS, 2, 3, cx, 2 * nb, LANES),
            VM(ROUNDS, 4, 3, nb, LANES), VM(ROUNDS, 4, 3, nb, LANES),
            VM(DESCENTS, 2, LANES), VM(DESCENTS, n, 2, LANES),
            VM(3, 2, cx, nb, LANES), VM(3, 2, cx + 4, nb, LANES), VM(2, cx + 4, nb, LANES),
            DMA(2, 2, 2), DMA(ROUNDS, 2, 2), DMA(2, 2, 2), DMA(ROUNDS, 2, 2),
            DMA(2, 4), DMA(ROUNDS, 4),
            DMA(DESCENTS), DMA(DESCENTS), DMA(2, 3), DMA(2, 3), DMA(4),
            pltpu.SemaphoreType.REGULAR((2,)),
        ],
        compiler_params=pltpu.CompilerParams(
            collective_id=0, has_side_effects=True, vmem_limit_bytes=limit
        ),
    )(stay(magnetic), stay(friction))
    return pl.pallas_call(
        functools.partial(finish_kernel, cx, cz, nb),
        out_shape=(shape, shape),
        in_specs=[inner] * 5,
        out_specs=(outer, outer),
        scratch_shapes=[
            VM(*magnetic.shape), VM(2, 3, step, cz, ny), pltpu.VMEM((2, 6 * step * cz, ny), jnp.bfloat16),
            DMA(cx // step), pltpu.SemaphoreType.DMA,
        ],
        compiler_params=pltpu.CompilerParams(vmem_limit_bytes=limit),
    )(relaxed, pot, induced, drag, back)


def solution(mesh):
    return jax.shard_map(
        body,
        mesh=mesh,
        in_specs=(P(None, "gx", "gz", "runs"), P("gz")),
        out_specs=(P(None, "gx", "gz", "runs"), P(None, "gx", "gz", "runs")),
        check_vma=False,
    )
```
